32 devices in a mesh: row: 8 (over z, y), col: 4 (over x, core).
Axes of the slice: x: 2, y: 2, z: 4, core: 2. Of those that a mesh axis runs over, the one named last changes fastest.
Arguments:
- atmo_states: float32 [10, 12, 128, 128], P(None, None, 'row'), may hold values from -6 to 6
- remap_weights: float32 [128, 16, 128, 128], P('row', 'col'), may hold values from -0.25 to 0.25
- intersection_tiles: int32 [128, 16], P('row', 'col'), may hold values from 0 to 47, as said below
- land_mask: int32 [128, 512], P('row', 'col'), may hold values 0 or 1
- ocean_state: float32 [3, 128, 512], P(None, 'row', 'col'), may hold values from -6 to 6
Outputs:
- flux_mean: float32 [10, 128, 512], P(None, 'row', 'col')
- final_state: float32 [3, 128, 512], P(None, 'row', 'col')
The draws below stay inside these ranges and needn't reach their ends.
Inputs may be any that keep to these rules, and one draw needn't show every extreme that they name: `intersection_tiles`: for every ocean row and block column, the first of its 4 slots names a tile of the previous row device (values below 16), the last one of the next row device (values from 32), the others of the own row device; row indices wrap around.
All inputs are finite; a program needn't handle non-finite values. No bound on the sum of `land_mask` on one device may be relied on, other than what follows from the above.
Results may differ from the reference program's by a relative error of at most 0.00017.
Values sent between devices are 32-bit elements; how exact they have to be, the bound alone decides.
No kernel may reach another device: no remote copies, remote signals or barrier semaphores. Data moves between devices by JAX's collectives and lax.ppermute only.
A program may use at most 64 MiB of HBM per device.

```python
import math
import jax
import jax.numpy as jnp
import numpy as np
from jax import lax

F = 10
K = 12
SUB = 6
TA = 128
KOV = 4
OC = 128
AT_DEV = 16
OR = 16
NAT = 128
NXO = 128
NYO = 512
N_ROW = 8
N_COL = 4


def draw_intersection_tiles(key, part):
    base = jax.random.randint(key, (NXO, N_COL, KOV), 0, AT_DEV, dtype=jnp.int32)
    base = base.at[0, 0, :].set(AT_DEV - 1)
    base = base.at[1, 0, :].set(0)
    slots = jnp.arange(KOV, dtype=jnp.int32)
    offsets = (jnp.minimum(slots, 1) + (slots == KOV - 1).astype(jnp.int32)) * AT_DEV
    return (base + offsets[None, None, :]).reshape(NXO, N_COL * KOV).astype(jnp.int32)


def place_ends(values, own_key, least, largest):
    dims = values.shape
    spot = [jax.random.randint(jax.random.fold_in(own_key, axis), (), 0, dims[axis]) for axis in range(len(dims))]
    values = values.at[tuple(spot)].set(least)
    longest = dims.index(max(dims))
    spot[longest] = (spot[longest] + 1) % dims[longest]
    return values.at[tuple(spot)].set(largest)


def steps_of(stream_key, extent, cuts, low, high):
    def one(axis_at, shards_of):
        draws = jax.random.uniform(jax.random.fold_in(jax.random.fold_in(stream_key, 6), axis_at), (shards_of,), jnp.float32, low / len(cuts), high / len(cuts))
        return jnp.repeat(jnp.exp(draws), extent[axis_at] // shards_of).reshape((-1,) + (1,) * (len(extent) - axis_at - 1))

    factor_of = one(*cuts[0])
    for cut in cuts[1:]:
        factor_of = factor_of * one(*cut)
    return factor_of


def noise(own_key, shape, scale, limit, split=(), held_as=jnp.bfloat16):
    entries = jax.random.normal(own_key, shape, jnp.float32) * scale
    if len(split) > 0:
        entries = steps_of(own_key, shape, split, -0.22, 0.18) * entries
    return jnp.clip(entries, min=-limit, max=limit).astype(held_as)


def setup_inputs(seed: int = 0) -> dict:
    streams_of = jax.random.split(jax.random.key(seed), 6)
    return {
        "atmo_states": noise(streams_of[0], (F, K, NAT, TA), 1.0, 6.0, ((2, 8),), jnp.float32),
        "remap_weights": noise(streams_of[1], (NXO, KOV * N_COL, TA, OC), (KOV * TA) ** -0.5, 0.25, ((0, 8), (1, 4)), jnp.float32),
        "intersection_tiles": draw_intersection_tiles(jax.random.fold_in(streams_of[5], 71), 0),
        "land_mask": place_ends((jax.random.randint(streams_of[3], (NXO, NYO), 0, 5) < 4).astype(jnp.int32), jax.random.fold_in(streams_of[3], 1), 0, 1),
        "ocean_state": noise(streams_of[4], (3, NXO, NYO), 1.0, 6.0, ((1, 8), (2, 4)), jnp.float32),
    }


def hermite_table(count_sub, count_levels):
    table = np.zeros((count_sub, count_levels))

    def add_slope(position_row, level, factor):
        if level == 0:
            table[position_row, 1] += factor
            table[position_row, 0] -= factor
        elif level == count_levels - 1:
            table[position_row, level] += factor
            table[position_row, level - 1] -= factor
        else:
            table[position_row, level + 1] += 0.5 * factor
            table[position_row, level - 1] -= 0.5 * factor

    for substep in range(count_sub):
        position = (substep + 0.5) * (count_levels - 1) / count_sub
        lower = min(int(math.floor(position)), count_levels - 2)
        fraction = position - lower
        table[substep, lower] += 2 * fraction ** 3 - 3 * fraction ** 2 + 1
        table[substep, lower + 1] += -2 * fraction ** 3 + 3 * fraction ** 2
        add_slope(substep, lower, fraction ** 3 - 2 * fraction ** 2 + fraction)
        add_slope(substep, lower + 1, fraction ** 3 - fraction ** 2)
    return table


def reference(atmo_states, remap_weights, intersection_tiles, land_mask, ocean_state):
    highest = lax.Precision.HIGHEST
    table = jnp.asarray(hermite_table(SUB, K), jnp.float32)
    interp = jnp.einsum("sk,fkta->fsta", table, atmo_states, precision=highest)
    owner = jnp.arange(OR * N_ROW, dtype=jnp.int32) // OR
    global_tiles = ((owner[:, None] * AT_DEV - AT_DEV + intersection_tiles) % (AT_DEV * N_ROW)).astype(jnp.int32)

    def one_row(items):
        tiles_row, weights_row = items
        picked = interp[:, :, tiles_row, :].reshape(F, SUB, N_COL, KOV, TA)
        weights_row = weights_row.reshape(N_COL, KOV, TA, OC)
        result = jnp.einsum("fscqa,cqao->fsco", picked, weights_row, precision=highest)
        return result.reshape(F, SUB, N_COL * OC)

    rows_out = lax.map(one_row, (global_tiles, remap_weights))
    forcing = jnp.transpose(rows_out, (2, 1, 0, 3))
    flux_mean = jnp.mean(forcing, axis=0)
    ocean = land_mask.astype(jnp.float32)
    height, zonal, merid = ocean_state[0], ocean_state[1], ocean_state[2]
    for substep in range(SUB):
        grad_x = (jnp.roll(height, -1, 0) - jnp.roll(height, 1, 0)) * 0.5
        zonal = ocean * (zonal - grad_x + 0.2 * merid + 0.5 * forcing[substep, 0])
        grad_y = (jnp.roll(height, -1, 1) - jnp.roll(height, 1, 1)) * 0.5
        merid = ocean * (merid - grad_y - 0.2 * zonal + 0.5 * forcing[substep, 1])
        spread = (jnp.roll(zonal, -1, 0) - jnp.roll(zonal, 1, 0)) * 0.5
        spread = spread + (jnp.roll(merid, -1, 1) - jnp.roll(merid, 1, 1)) * 0.5
        height = height - spread + 0.5 * forcing[substep, 2]
    return flux_mean, jnp.stack([height, zonal, merid])
```

```python
import functools
import math

import jax
import jax.numpy as jnp
import numpy as np
from jax import lax
from jax.experimental import pallas as pl
from jax.experimental.pallas import tpu as pltpu
from jax.sharding import PartitionSpec as P

SUB = 6
DYN = 3


def hermite_table(count_sub, count_levels):
    table = np.zeros((count_sub, count_levels))

    def add_slope(position_row, level, factor):
        if level == 0:
            table[position_row, 1] += factor
            table[position_row, 0] -= factor
        elif level == count_levels - 1:
            table[position_row, level] += factor
            table[position_row, level - 1] -= factor
        else:
            table[position_row, level + 1] += 0.5 * factor
            table[position_row, level - 1] -= 0.5 * factor

    for substep in range(count_sub):
        position = (substep + 0.5) * (count_levels - 1) / count_sub
        lower = min(int(math.floor(position)), count_levels - 2)
        fraction = position - lower
        table[substep, lower] += 2 * fraction**3 - 3 * fraction**2 + 1
        table[substep, lower + 1] += -2 * fraction**3 + 3 * fraction**2
        add_slope(substep, lower, fraction**3 - 2 * fraction**2 + fraction)
        add_slope(substep, lower + 1, fraction**3 - fraction**2)
    return table


WIDTHS = [2 * (SUB - s) - (1 if f < 2 else 2) for s in range(SUB) for f in range(DYN)]
WIDTHS += [2 * SUB, 2 * SUB - 1, 2 * SUB - 1, 2 * SUB - 1]
PLANES = SUB * DYN
ITEMS = len(WIDTHS)
ROW_AT = np.concatenate([[0], np.cumsum(WIDTHS)]).tolist()
LANE_AT = ROW_AT[:PLANES] + [ROW_AT[i] - ROW_AT[PLANES] for i in range(PLANES, ITEMS)]
MAIN = -(-ROW_AT[-1] // 8) * 8
GROUPS = 2


def interp_kernel(table, mean, rows, atmo_ref, out_ref):
    fields, levels, tiles, _ = atmo_ref.shape
    for f in range(DYN):
        level = [atmo_ref[f, k] for k in range(levels)]
        for s in range(SUB):
            terms = [float(table[s, k]) * level[k] for k in range(levels) if table[s, k] != 0]
            out_ref[pl.ds(s * DYN + f, tiles, stride=rows), :] = functools.reduce(jnp.add, terms)
    for f in range(DYN, fields):
        terms = [float(mean[k]) * atmo_ref[f, k] for k in range(levels)]
        out_ref[pl.ds(PLANES + f - DYN, tiles, stride=rows), :] = functools.reduce(jnp.add, terms)
    pad = out_ref.shape[0] - tiles * rows
    out_ref[tiles * rows :, :] = jnp.zeros((pad, out_ref.shape[1]), jnp.float32)


def split_tiles(source_ref, split_ref, base, tiles, rows):
    for g in range(tiles):
        value = source_ref[g * rows : g * rows + 32, :]
        high = value.astype(jnp.bfloat16)
        split_ref[base + g, 0:32, :] = high
        split_ref[base + g, 32:64, :] = (value - high.astype(jnp.float32)).astype(jnp.bfloat16)


def remap_row(split_ref, first, second, wa, wb):
    left = jnp.concatenate([split_ref[first], split_ref[second]], axis=1)
    weights = jnp.concatenate([wa, wb], axis=0)
    high = weights.astype(jnp.bfloat16)
    low = (weights - high.astype(jnp.float32)).astype(jnp.bfloat16)
    both = jnp.dot(left, high, preferred_element_type=jnp.float32)
    return both[0:32] + both[32:64] + jnp.dot(left[0:32], low, preferred_element_type=jnp.float32)


def own_kernel(rows, tiles_ref, own_ref, wa_ref, wb_ref, acc_ref, split_ref):
    step = pl.program_id(0)
    per = wa_ref.shape[0]
    slots = 4

    @pl.when(step == 0)
    def _():
        split_tiles(own_ref, split_ref, 0, split_ref.shape[0], rows)

    for x in range(per):
        at = (step * per + x) * slots
        tiles = split_ref.shape[0]
        first, second = tiles_ref[at + 1] - tiles, tiles_ref[at + 2] - tiles
        acc_ref[:, x, :] = remap_row(split_ref, first, second, wa_ref[x, 0], wb_ref[x, 0])


def rim_kernel(rows, tiles_ref, odd_ref, one_ref, two_ref, wa_ref, wb_ref, own_ref, state_ref, mask_ref,
               force_ref, mean_ref, main1_ref, main2_ref, edge1_ref, edge2_ref, split_ref, total_ref):
    step = pl.program_id(0)
    per = wa_ref.shape[0]
    slots = 4
    tiles = split_ref.shape[0] // 2
    row_odd, col_odd = odd_ref[0], odd_ref[1]

    @pl.when(step == 0)
    def _():
        split_tiles(one_ref, split_ref, 0, tiles, rows)
        split_tiles(two_ref, split_ref, tiles, tiles, rows)

    for x in range(per):
        at = (step * per + x) * slots
        first = tiles_ref[at] + tiles * (1 - row_odd)
        second = tiles_ref[at + 3] - 2 * tiles + tiles * row_odd
        value = remap_row(split_ref, first, second, wa_ref[x, 0], wb_ref[x, 0])
        total_ref[step, :, x, :] = value + own_ref[:, x, :]

    @pl.when(step == pl.num_programs(0) - 1)
    def _():
        plane = [jnp.concatenate([total_ref[k, j] for k in range(total_ref.shape[0])], axis=0) for j in range(rows)]
        for p in range(PLANES):
            force_ref[p] = plane[p]
        for f in range(DYN):
            mean_ref[f] = functools.reduce(jnp.add, [plane[s * DYN + f] for s in range(SUB)]) * (1.0 / SUB)
        for f in range(DYN, mean_ref.shape[0]):
            mean_ref[f] = plane[PLANES + f - DYN]
        items = plane[:PLANES] + [state_ref[k] for k in range(DYN)] + [mask_ref[...].astype(jnp.float32)]
        high = items[0].shape[0]
        wide = items[0].shape[1]

        def pack(down_ref, up_ref):
            for i, value in enumerate(items):
                w = WIDTHS[i]
                if w:
                    down_ref[ROW_AT[i] : ROW_AT[i] + w, :] = value[high - w :]
                    up_ref[ROW_AT[i] : ROW_AT[i] + w, :] = value[:w]
            for ref in (down_ref, up_ref):
                ref[ROW_AT[-1] :, :] = jnp.zeros((MAIN - ROW_AT[-1], wide), jnp.float32)

        @pl.when(row_odd == 0)
        def _():
            pack(main1_ref, main2_ref)

        @pl.when(row_odd != 0)
        def _():
            pack(main2_ref, main1_ref)

        lane = lax.broadcasted_iota(jnp.int32, (high, wide), 1)
        for g, group in enumerate((range(PLANES), range(PLANES, ITEMS))):
            last = jnp.zeros((high, wide), jnp.float32)
            head = jnp.zeros((high, wide), jnp.float32)
            for i in group:
                w, at = WIDTHS[i], LANE_AT[i]
                if w:
                    last = jnp.where(lane >= at, pltpu.roll(items[i], (at + w) % wide, 1), last)
                    head = jnp.where(lane >= at, pltpu.roll(items[i], at, 1), head)
            edge1_ref[g * high : (g + 1) * high, :] = jnp.where(col_odd == 0, last, head)
            edge2_ref[g * high : (g + 1) * high, :] = jnp.where(col_odd == 0, head, last)


def ocean_kernel(odd_ref, force_ref, state_ref, mask_ref, edge1_ref, edge2_ref, one_ref, two_ref, out_ref, top_ref, low_ref):
    row_odd, col_odd = odd_ref[0], odd_ref[1]
    high, wide = mask_ref.shape
    top_ref[...] = jnp.where(row_odd == 0, two_ref[...], one_ref[...])
    low_ref[...] = jnp.where(row_odd == 0, one_ref[...], two_ref[...])
    rim = GROUPS * high
    second = rim + MAIN
    lane = lax.broadcasted_iota(jnp.int32, (3 * high, wide), 1)

    def edges(g):
        own = slice(g * high, (g + 1) * high)
        far = slice(second + g * high, second + (g + 1) * high)
        a = jnp.concatenate([top_ref[own], edge1_ref[own], low_ref[own]], axis=0)
        b = jnp.concatenate([top_ref[far], edge2_ref[own], low_ref[far]], axis=0)
        return jnp.where(col_odd == 0, b, a), jnp.where(col_odd == 0, a, b)

    sides = [edges(g) for g in range(GROUPS)]

    def extended(i, own):
        w, at = WIDTHS[i], LANE_AT[i]
        start = rim + ROW_AT[i]
        main = jnp.concatenate([top_ref[start + w - high : start + w, :], own, low_ref[start : start + high, :]], axis=0)
        left, right = sides[0 if i < PLANES else 1]
        edge = jnp.where(lane < wide // 2, pltpu.roll(right, (wide - at) % wide, 1), pltpu.roll(left, (2 * wide - w - at) % wide, 1))
        return jnp.concatenate([main, edge], axis=1)

    rows, lanes = 3 * high, 2 * wide
    before = lambda v, axis: pltpu.roll(v, 1, axis)
    after = lambda v, axis: pltpu.roll(v, (rows, lanes)[axis] - 1, axis)
    height = extended(PLANES, state_ref[0])
    zonal = extended(PLANES + 1, state_ref[1])
    merid = extended(PLANES + 2, state_ref[2])
    ocean = extended(PLANES + 3, mask_ref[...].astype(jnp.float32))
    for s in range(SUB):
        push_u, push_v, push_h = (extended(s * DYN + f, force_ref[s * DYN + f]) for f in range(DYN))
        grad_x = (after(height, 0) - before(height, 0)) * 0.5
        grad_y = (after(height, 1) - before(height, 1)) * 0.5
        zonal = ocean * (zonal - grad_x + 0.2 * merid + 0.5 * push_u)
        merid = ocean * (merid - grad_y - 0.2 * zonal + 0.5 * push_v)
        spread = (after(zonal, 0) - before(zonal, 0)) * 0.5 + (after(merid, 1) - before(merid, 1)) * 0.5
        height = height - spread + 0.5 * push_h
    for k, value in enumerate((height, zonal, merid)):
        out_ref[k] = value[high : 2 * high, :wide]


def per_device(size_row, size_col, atmo_states, remap_weights, intersection_tiles, land_mask, ocean_state):
    fields, levels, tiles, cells = atmo_states.shape
    high, wide = land_mask.shape
    rows = PLANES + fields - DYN
    vmem = pl.BlockSpec(memory_space=pltpu.VMEM)
    smem = pl.BlockSpec(memory_space=pltpu.SMEM)
    f32 = lambda *shape: jax.ShapeDtypeStruct(shape, jnp.float32)
    params = lambda: pltpu.CompilerParams(vmem_limit_bytes=32 << 20)

    def pairs(size):
        near = [(i, i ^ 1) for i in range(size)]
        far = [(i, (i + 1) % size if i % 2 else (i - 1) % size) for i in range(size)]
        return near, far

    row_near, row_far = pairs(size_row)
    col_near, col_far = pairs(size_col)
    odd = jnp.stack([lax.axis_index("row") % 2, lax.axis_index("col") % 2]).astype(jnp.int32)
    flat_tiles = intersection_tiles.reshape(-1)

    table = hermite_table(SUB, levels).astype(np.float32)
    mean = table.astype(np.float64).mean(axis=0)
    own = pl.pallas_call(
        functools.partial(interp_kernel, table, mean, rows),
        out_shape=f32(tiles * rows + 8, cells),
        in_specs=[vmem],
        out_specs=vmem,
        compiler_params=params(),
    )(atmo_states)
    two = lax.ppermute(own, "row", row_far)
    one = lax.ppermute(own, "row", row_near)

    steps = 2
    per = high // steps
    weight = lambda slot: pl.BlockSpec((per, 1, cells, wide), lambda i, *_: (i, slot, 0, 0))
    whole = lambda *shape: pl.BlockSpec(shape, lambda i, *_: (0,) * len(shape))
    split = pltpu.VMEM((tiles, 64, cells), jnp.bfloat16)
    length = tiles * rows + 8
    acc = pl.pallas_call(
        functools.partial(own_kernel, rows),
        out_shape=f32(32, high, wide),
        grid_spec=pltpu.PrefetchScalarGridSpec(
            num_scalar_prefetch=1,
            grid=(steps,),
            in_specs=[whole(length, cells), weight(1), weight(2)],
            out_specs=pl.BlockSpec((32, per, wide), lambda i, *_: (0, i, 0)),
            scratch_shapes=[split],
        ),
        compiler_params=params(),
        cost_estimate=pl.CostEstimate(flops=10**9, bytes_accessed=4 << 20, transcendentals=0),
    )(flat_tiles, own, remap_weights, remap_weights)

    force, flux_mean, main1, main2, edge1, edge2 = pl.pallas_call(
        functools.partial(rim_kernel, rows),
        out_shape=(f32(PLANES, high, wide), f32(fields, high, wide), f32(MAIN, wide), f32(MAIN, wide),
                   f32(GROUPS * high, wide), f32(GROUPS * high, wide)),
        grid_spec=pltpu.PrefetchScalarGridSpec(
            num_scalar_prefetch=2,
            grid=(steps,),
            in_specs=[whole(length, cells), whole(length, cells), weight(0), weight(3),
                      pl.BlockSpec((32, per, wide), lambda i, *_: (0, i, 0)),
                      whole(3, high, wide), whole(high, wide)],
            out_specs=(whole(PLANES, high, wide), whole(fields, high, wide), whole(MAIN, wide), whole(MAIN, wide),
                       whole(GROUPS * high, wide), whole(GROUPS * high, wide)),
            scratch_shapes=[pltpu.VMEM((2 * tiles, 64, cells), jnp.bfloat16), pltpu.VMEM((steps, 32, per, wide), jnp.float32)],
        ),
        compiler_params=params(),
        cost_estimate=pl.CostEstimate(flops=10**9, bytes_accessed=4 << 20, transcendentals=0),
    )(flat_tiles, odd, one, two, remap_weights, remap_weights, acc, ocean_state, land_mask)

    from2 = lax.ppermute(edge2, "col", col_far)
    from1 = lax.ppermute(edge1, "col", col_near)
    join = lambda main: jnp.concatenate([from1, main, from2], axis=0)
    rim2 = lax.ppermute(join(main2), "row", row_far)
    rim1 = lax.ppermute(join(main1), "row", row_near)

    length = 2 * GROUPS * high + MAIN
    final = pl.pallas_call(
        ocean_kernel,
        out_shape=f32(3, high, wide),
        in_specs=[smem] + [vmem] * 7,
        out_specs=vmem,
        scratch_shapes=[pltpu.VMEM((length, wide), jnp.float32)] * 2,
        compiler_params=params(),
    )(odd, force, ocean_state, land_mask, from1, from2, rim1, rim2)
    return flux_mean, final


def solution(mesh):
    placed = (
        P(None, None, "row", None),
        P("row", "col", None, None),
        P("row", "col"),
        P("row", "col"),
        P(None, "row", "col"),
    )
    return jax.shard_map(
        functools.partial(per_device, mesh.shape["row"], mesh.shape["col"]),
        mesh=mesh,
        in_specs=placed,
        out_specs=(P(None, "row", "col"), P(None, "row", "col")),
        check_vma=False,
    )
```

```python
import functools
import math

import jax
import jax.numpy as jnp
import numpy as np
from jax import lax
from jax.experimental import pallas as pl
from jax.experimental.pallas import tpu as pltpu
from jax.sharding import PartitionSpec as P

SUB = 6
DYN = 3


def hermite_table(count_sub, count_levels):
    table = np.zeros((count_sub, count_levels))

    def add_slope(position_row, level, factor):
        if level == 0:
            table[position_row, 1] += factor
            table[position_row, 0] -= factor
        elif level == count_levels - 1:
            table[position_row, level] += factor
            table[position_row, level - 1] -= factor
        else:
            table[position_row, level + 1] += 0.5 * factor
            table[position_row, level - 1] -= 0.5 * factor

    for substep in range(count_sub):
        position = (substep + 0.5) * (count_levels - 1) / count_sub
        lower = min(int(math.floor(position)), count_levels - 2)
        fraction = position - lower
        table[substep, lower] += 2 * fraction**3 - 3 * fraction**2 + 1
        table[substep, lower + 1] += -2 * fraction**3 + 3 * fraction**2
        add_slope(substep, lower, fraction**3 - 2 * fraction**2 + fraction)
        add_slope(substep, lower + 1, fraction**3 - fraction**2)
    return table


WIDTHS = [2 * (SUB - s) - (1 if f < 2 else 2) for s in range(SUB) for f in range(DYN)]
WIDTHS += [2 * SUB, 2 * SUB - 1, 2 * SUB - 1, 2 * SUB - 1]
PLANES = SUB * DYN
ITEMS = len(WIDTHS)
ROW_AT = np.concatenate([[0], np.cumsum(WIDTHS)]).tolist()
LANE_AT = ROW_AT[:PLANES] + [ROW_AT[i] - ROW_AT[PLANES] for i in range(PLANES, ITEMS)]
CORNERS = [max(w - 1, 0) for w in WIDTHS]
CORNER_AT = np.concatenate([[0], np.cumsum(CORNERS)]).tolist()
MAIN = -(-ROW_AT[-1] // 8) * 8
GROUPS = 3


def interp_kernel(table, mean, rows, atmo_ref, out_ref, half_ref):
    fields, levels, tiles, _ = atmo_ref.shape
    for f in range(fields):
        level = [atmo_ref[f, k] for k in range(levels)]
        if f < DYN:
            for s in range(SUB):
                terms = [float(table[s, k]) * level[k] for k in range(levels) if table[s, k] != 0]
                out_ref[pl.ds(s * DYN + f, tiles, stride=rows), :] = functools.reduce(jnp.add, terms)
        else:
            terms = [float(mean[k]) * level[k] for k in range(levels)]
            out_ref[pl.ds(PLANES + f - DYN, tiles, stride=rows), :] = functools.reduce(jnp.add, terms)
    part = half_ref.shape[0]
    half_ref[...] = out_ref[pl.ds(pl.multiple_of(lax.axis_index("col") % 2 * part, 8), part), :]


def split_tiles(source_ref, split_ref, base, rows):
    tiles = source_ref.shape[0] // rows
    for g in range(tiles):
        value = source_ref[g * rows : min(g * rows + 32, source_ref.shape[0]), :]
        if value.shape[0] < 32:
            value = jnp.concatenate([value, jnp.zeros((32 - value.shape[0], value.shape[1]), value.dtype)], axis=0)
        high = value.astype(jnp.bfloat16)
        split_ref[base + g, 0:32, :] = high
        split_ref[base + g, 32:64, :] = (value - high.astype(jnp.float32)).astype(jnp.bfloat16)


def split_weights(wa, wb):
    weights = jnp.concatenate([wa, wb], axis=0)
    high = weights.astype(jnp.bfloat16)
    low = (weights - high.astype(jnp.float32)).astype(jnp.bfloat16)
    return jnp.concatenate([high, low], axis=1)


def remap_row(split_ref, first, second, weights):
    left = jnp.concatenate([split_ref[first], split_ref[second]], axis=1)
    both = jnp.dot(left, weights, preferred_element_type=jnp.float32)
    wide = weights.shape[1] // 2
    return both[0:32, :wide] + both[32:64, :wide] + both[0:32, wide:]


def own_kernel(rows, tiles_ref, own_ref, weight_ref, acc_ref, rest_ref, split_ref):
    index = tiles_ref[...] - split_ref.shape[0]
    split_tiles(own_ref, split_ref, 0, rows)
    for x in range(weight_ref.shape[0]):
        first, second = index[1, x], index[2, x]
        weights = split_weights(weight_ref[x, 1], weight_ref[x, 2])
        acc_ref[:, x, :] = remap_row(split_ref, first, second, weights)
        rest_ref[x] = split_weights(weight_ref[x, 0], weight_ref[x, 3])


def rim_kernel(rows, tiles_ref, two_far_ref, two_ref, one_far_ref, one_ref, rest_ref, own_ref, state_ref, mask_ref,
               total_ref, main1_ref, main2_ref, edge1_ref, edge2_ref, split_ref):
    part = split_ref.shape[0] // 4
    for k, ref in enumerate((one_ref, one_far_ref, two_ref, two_far_ref)):
        split_tiles(ref, split_ref, k * part, rows)
    row_odd, col_odd = lax.axis_index("row") % 2, lax.axis_index("col") % 2
    names = tiles_ref[...]
    place = lambda name: name % part + part * ((name // part + col_odd) % 2)
    before = place(names) + 2 * part * (1 - row_odd)
    after = place(names - 4 * part) + 2 * part * row_odd
    for x in range(rest_ref.shape[0]):
        total_ref[:, x, :] = remap_row(split_ref, before[0, x], after[3, x], rest_ref[x]) + own_ref[:, x, :]

    items = [total_ref[p] for p in range(PLANES)] + [state_ref[k] for k in range(DYN)] + [mask_ref[...].astype(jnp.float32)]
    high, wide = mask_ref.shape
    row_even, col_even = row_odd == 0, col_odd == 0

    for i, value in enumerate(items):
        w, at = WIDTHS[i], ROW_AT[i]
        if w:
            down, up = value[high - w :], value[:w]
            main1_ref[at : at + w, :] = jnp.where(row_even, down, up)
            main2_ref[at : at + w, :] = jnp.where(row_even, up, down)
    for ref in (main1_ref, main2_ref):
        ref[ROW_AT[-1] :, :] = jnp.zeros((MAIN - ROW_AT[-1], wide), jnp.float32)

    lane = lax.broadcasted_iota(jnp.int32, (high, wide), 1)
    groups = ((range(PLANES), WIDTHS, LANE_AT), (range(PLANES, ITEMS), WIDTHS, LANE_AT), (range(ITEMS), CORNERS, CORNER_AT))
    for g, (members, widths, places) in enumerate(groups):
        last = jnp.zeros((high, wide), jnp.float32)
        head = jnp.zeros((high, wide), jnp.float32)
        for i in members:
            w, at = widths[i], places[i]
            if w:
                last = jnp.where(lane >= at, pltpu.roll(items[i], (at + w) % wide, 1), last)
                head = jnp.where(lane >= at, pltpu.roll(items[i], at, 1), head)
        edge1_ref[g * high : (g + 1) * high, :] = jnp.where(col_even, last, head)
        edge2_ref[g * high : (g + 1) * high, :] = jnp.where(col_even, head, last)


def ocean_kernel(force_ref, state_ref, mask_ref, edge1_ref, edge2_ref, two_ref, one_ref, out_ref, top_ref, low_ref):
    high, wide = mask_ref.shape
    row_even, col_even = lax.axis_index("row") % 2 == 0, lax.axis_index("col") % 2 == 0
    one, two = one_ref[...], two_ref[...]
    top_ref[...] = jnp.where(row_even, two, one)
    low_ref[...] = jnp.where(row_even, one, two)
    second = high + MAIN
    lane = lax.broadcasted_iota(jnp.int32, (high, wide), 1)

    def sides(a, b):
        return jnp.where(col_even, b, a), jnp.where(col_even, a, b)

    beside = [sides(edge1_ref[g * high : (g + 1) * high], edge2_ref[g * high : (g + 1) * high]) for g in range(2)]
    above = sides(top_ref[:high], top_ref[second:])
    below = sides(low_ref[:high], low_ref[second:])

    def edge(pair, w, at):
        left, right = pair
        if w == 0:
            return jnp.zeros_like(left)
        return jnp.where(lane < wide // 2, pltpu.roll(right, (wide - at) % wide, 1), pltpu.roll(left, (2 * wide - w - at) % wide, 1))

    def extended(i, own, rim):
        w, start = WIDTHS[i], high + ROW_AT[i]
        main = [top_ref[start + w - rim : start + w, :], own, low_ref[start : start + rim, :]]
        rest = [
            edge(above, CORNERS[i], CORNER_AT[i])[high - rim :],
            edge(beside[0 if i < PLANES else 1], w, LANE_AT[i]),
            edge(below, CORNERS[i], CORNER_AT[i])[:rim],
        ]
        return jnp.concatenate([jnp.concatenate(main, axis=0), jnp.concatenate(rest, axis=0)], axis=1)

    before = lambda v, axis: pltpu.roll(v, 1, axis)
    after = lambda v, axis: pltpu.roll(v, v.shape[axis] - 1, axis)
    rim = high
    height = extended(PLANES, state_ref[0], rim)
    zonal = extended(PLANES + 1, state_ref[1], rim)
    merid = extended(PLANES + 2, state_ref[2], rim)
    ocean = extended(PLANES + 3, mask_ref[...].astype(jnp.float32), rim)
    for s in range(SUB):
        reach = -(-2 * (SUB - s) // 8) * 8
        if reach < rim:
            cut = rim - reach
            height, zonal, merid, ocean = (v[cut : v.shape[0] - cut] for v in (height, zonal, merid, ocean))
            rim = reach
        push_u, push_v, push_h = (extended(s * DYN + f, force_ref[s * DYN + f], rim) for f in range(DYN))
        grad_x = (after(height, 0) - before(height, 0)) * 0.5
        grad_y = (after(height, 1) - before(height, 1)) * 0.5
        zonal = ocean * (zonal - grad_x + 0.2 * merid + 0.5 * push_u)
        merid = ocean * (merid - grad_y - 0.2 * zonal + 0.5 * push_v)
        spread = (after(zonal, 0) - before(zonal, 0)) * 0.5 + (after(merid, 1) - before(merid, 1)) * 0.5
        height = height - spread + 0.5 * push_h
    for k, value in enumerate((height, zonal, merid)):
        out_ref[k] = value[rim : rim + high, :wide]


def per_device(size_row, size_col, atmo_states, remap_weights, intersection_tiles, land_mask, ocean_state):
    fields, levels, tiles, cells = atmo_states.shape
    high, wide = land_mask.shape
    rows = PLANES + fields - DYN
    vmem = pl.BlockSpec(memory_space=pltpu.VMEM)
    f32 = lambda *shape: jax.ShapeDtypeStruct(shape, jnp.float32)
    params = lambda: pltpu.CompilerParams(vmem_limit_bytes=32 << 20)

    def pairs(size):
        near = [(i, i ^ 1) for i in range(size)]
        far = [(i, (i + 1) % size if i % 2 else (i - 1) % size) for i in range(size)]
        return near, far

    row_near, row_far = pairs(size_row)
    col_near, col_far = pairs(size_col)
    half = tiles // 2
    names = intersection_tiles.T

    table = hermite_table(SUB, levels).astype(np.float32)
    mean = table.astype(np.float64).mean(axis=0)
    own, part = pl.pallas_call(
        functools.partial(interp_kernel, table, mean, rows),
        out_shape=(f32(tiles * rows, cells), f32(half * rows, cells)),
        in_specs=[vmem],
        out_specs=(vmem, vmem),
        compiler_params=params(),
        cost_estimate=pl.CostEstimate(flops=10**10, bytes_accessed=4 << 20, transcendentals=0),
    )(atmo_states)
    one = lax.ppermute(part, "row", row_near)
    two = lax.ppermute(part, "row", row_far)

    acc, rest = pl.pallas_call(
        functools.partial(own_kernel, rows),
        out_shape=(f32(32, high, wide), jax.ShapeDtypeStruct((high, 2 * cells, 2 * wide), jnp.bfloat16)),
        in_specs=[vmem] * 3,
        out_specs=(vmem, vmem),
        scratch_shapes=[pltpu.VMEM((tiles, 64, cells), jnp.bfloat16)],
        compiler_params=params(),
        cost_estimate=pl.CostEstimate(flops=10**9, bytes_accessed=4 << 20, transcendentals=0),
    )(names, own, remap_weights)

    two, one, acc, rest = lax.optimization_barrier((two, one, acc, rest))
    one_far = lax.ppermute(one, "col", col_near)
    two_far = lax.ppermute(two, "col", col_near)

    total, main1, main2, edge1, edge2 = pl.pallas_call(
        functools.partial(rim_kernel, rows),
        out_shape=(f32(32, high, wide), f32(MAIN, wide), f32(MAIN, wide), f32(GROUPS * high, wide), f32(GROUPS * high, wide)),
        in_specs=[vmem] * 9,
        out_specs=(vmem,) * 5,
        scratch_shapes=[pltpu.VMEM((2 * tiles, 64, cells), jnp.bfloat16)],
        compiler_params=params(),
        cost_estimate=pl.CostEstimate(flops=10**9, bytes_accessed=4 << 20, transcendentals=0),
    )(names, two_far, two, one_far, one, rest, acc, ocean_state, land_mask)
    forced = total[:PLANES].reshape(SUB, DYN, high, wide)
    flux_mean = jnp.concatenate([jnp.mean(forced, axis=0), total[PLANES:rows]], axis=0)

    from2 = lax.ppermute(edge2, "col", col_far)
    from1 = lax.ppermute(edge1, "col", col_near)
    join = lambda main: jnp.concatenate([from1[2 * high :], main, from2[2 * high :]], axis=0)
    rim2 = lax.ppermute(join(main2), "row", row_far)
    rim1 = lax.ppermute(join(main1), "row", row_near)

    length = 2 * high + MAIN
    final = pl.pallas_call(
        ocean_kernel,
        out_shape=f32(3, high, wide),
        in_specs=[vmem] * 7,
        out_specs=vmem,
        scratch_shapes=[pltpu.VMEM((length, wide), jnp.float32)] * 2,
        compiler_params=params(),
    )(total, ocean_state, land_mask, from1, from2, rim2, rim1)
    return flux_mean, final


def solution(mesh):
    placed = (
        P(None, None, "row", None),
        P("row", "col", None, None),
        P("row", "col"),
        P("row", "col"),
        P(None, "row", "col"),
    )
    return jax.shard_map(
        functools.partial(per_device, mesh.shape["row"], mesh.shape["col"]),
        mesh=mesh,
        in_specs=placed,
        out_specs=(P(None, "row", "col"), P(None, "row", "col")),
        check_vma=False,
    )
```

```python
import functools
import math

import jax
import jax.numpy as jnp
import numpy as np
from jax import lax
from jax.experimental import pallas as pl
from jax.experimental.pallas import tpu as pltpu
from jax.sharding import PartitionSpec as P

SUB = 6
DYN = 3


def hermite_table(count_sub, count_levels):
    table = np.zeros((count_sub, count_levels))

    def add_slope(position_row, level, factor):
        if level == 0:
            table[position_row, 1] += factor
            table[position_row, 0] -= factor
        elif level == count_levels - 1:
            table[position_row, level] += factor
            table[position_row, level - 1] -= factor
        else:
            table[position_row, level + 1] += 0.5 * factor
            table[position_row, level - 1] -= 0.5 * factor

    for substep in range(count_sub):
        position = (substep + 0.5) * (count_levels - 1) / count_sub
        lower = min(int(math.floor(position)), count_levels - 2)
        fraction = position - lower
        table[substep, lower] += 2 * fraction**3 - 3 * fraction**2 + 1
        table[substep, lower + 1] += -2 * fraction**3 + 3 * fraction**2
        add_slope(substep, lower, fraction**3 - 2 * fraction**2 + fraction)
        add_slope(substep, lower + 1, fraction**3 - fraction**2)
    return table


WIDTHS = [2 * (SUB - s) - (1 if f < 2 else 2) for s in range(SUB) for f in range(DYN)]
WIDTHS += [2 * SUB, 2 * SUB - 1, 2 * SUB - 1, 2 * SUB - 1]
PLANES = SUB * DYN
ITEMS = len(WIDTHS)
ROW_AT = np.concatenate([[0], np.cumsum(WIDTHS)]).tolist()
LANE_AT = ROW_AT[:PLANES] + [ROW_AT[i] - ROW_AT[PLANES] for i in range(PLANES, ITEMS)]
CORNERS = [max(w - 1, 0) for w in WIDTHS]
CORNER_AT = np.concatenate([[0], np.cumsum(CORNERS)]).tolist()
MAIN = -(-ROW_AT[-1] // 8) * 8
GROUPS = 3


def interp_kernel(table, mean, rows, atmo_ref, out_ref, half_ref):
    fields, levels, tiles, _ = atmo_ref.shape
    for f in range(fields):
        level = [atmo_ref[f, k] for k in range(levels)]
        if f < DYN:
            for s in range(SUB):
                terms = [float(table[s, k]) * level[k] for k in range(levels) if table[s, k] != 0]
                out_ref[pl.ds(s * DYN + f, tiles, stride=rows), :] = functools.reduce(jnp.add, terms)
        else:
            terms = [float(mean[k]) * level[k] for k in range(levels)]
            out_ref[pl.ds(PLANES + f - DYN, tiles, stride=rows), :] = functools.reduce(jnp.add, terms)
    part = half_ref.shape[0]
    half_ref[...] = out_ref[pl.ds(pl.multiple_of(lax.axis_index("col") % 2 * part, 8), part), :]


def split_tiles(source_ref, split_ref, base, rows):
    tiles = source_ref.shape[0] // rows
    for g in range(tiles):
        value = source_ref[g * rows : min(g * rows + 32, source_ref.shape[0]), :]
        if value.shape[0] < 32:
            value = jnp.concatenate([value, jnp.zeros((32 - value.shape[0], value.shape[1]), value.dtype)], axis=0)
        high = value.astype(jnp.bfloat16)
        split_ref[base + g, 0:32, :] = high
        split_ref[base + g, 32:64, :] = (value - high.astype(jnp.float32)).astype(jnp.bfloat16)


def split_weights(wa, wb):
    weights = jnp.concatenate([wa, wb], axis=0)
    high = weights.astype(jnp.bfloat16)
    low = (weights - high.astype(jnp.float32)).astype(jnp.bfloat16)
    return jnp.concatenate([high, low], axis=1)


def remap_row(split_ref, first, second, weights):
    left = jnp.concatenate([split_ref[first], split_ref[second]], axis=1)
    both = jnp.dot(left, weights, preferred_element_type=jnp.float32)
    wide = weights.shape[1] // 2
    return both[0:32, :wide] + both[32:64, :wide] + both[0:32, wide:]


def own_kernel(rows, tiles_ref, own_ref, weight_ref, acc_ref, rest_ref, split_ref):
    index = tiles_ref[...] - split_ref.shape[0]
    split_tiles(own_ref, split_ref, 0, rows)
    for x in range(weight_ref.shape[0]):
        first, second = index[1, x], index[2, x]
        weights = split_weights(weight_ref[x, 1], weight_ref[x, 2])
        acc_ref[:, x, :] = remap_row(split_ref, first, second, weights)
        rest_ref[x] = split_weights(weight_ref[x, 0], weight_ref[x, 3])


def rim_kernel(rows, tiles_ref, near_ref, far_ref, rest_ref, own_ref, state_ref, mask_ref,
               total_ref, down_ref, up_ref, edge1_ref, edge2_ref, split_ref):
    part = split_ref.shape[0] // 4
    for side in range(2):
        split_tiles(near_ref.at[side], split_ref, 2 * side * part, rows)
        split_tiles(far_ref.at[side], split_ref, (2 * side + 1) * part, rows)
    col_odd = lax.axis_index("col") % 2
    names = tiles_ref[...]
    place = lambda name: name % part + part * ((name // part + col_odd) % 2)
    before, after = place(names), place(names - 4 * part) + 2 * part
    for x in range(rest_ref.shape[0]):
        total_ref[:, x, :] = remap_row(split_ref, before[0, x], after[3, x], rest_ref[x]) + own_ref[:, x, :]

    items = [total_ref[p] for p in range(PLANES)] + [state_ref[k] for k in range(DYN)] + [mask_ref[...].astype(jnp.float32)]
    high, wide = mask_ref.shape
    col_even = col_odd == 0

    for i, value in enumerate(items):
        w, at = WIDTHS[i], ROW_AT[i]
        if w:
            down_ref[at : at + w, :] = value[high - w :]
            up_ref[at : at + w, :] = value[:w]
    for ref in (down_ref, up_ref):
        ref[ROW_AT[-1] :, :] = jnp.zeros((MAIN - ROW_AT[-1], wide), jnp.float32)

    lane = lax.broadcasted_iota(jnp.int32, (high, wide), 1)
    groups = ((range(PLANES), WIDTHS, LANE_AT), (range(PLANES, ITEMS), WIDTHS, LANE_AT), (range(ITEMS), CORNERS, CORNER_AT))
    for g, (members, widths, places) in enumerate(groups):
        last = jnp.zeros((high, wide), jnp.float32)
        head = jnp.zeros((high, wide), jnp.float32)
        for i in members:
            w, at = widths[i], places[i]
            if w:
                last = jnp.where(lane >= at, pltpu.roll(items[i], (at + w) % wide, 1), last)
                head = jnp.where(lane >= at, pltpu.roll(items[i], at, 1), head)
        edge1_ref[g * high : (g + 1) * high, :] = jnp.where(col_even, last, head)
        edge2_ref[g * high : (g + 1) * high, :] = jnp.where(col_even, head, last)


def ocean_kernel(force_ref, state_ref, mask_ref, edge1_ref, edge2_ref, low_ref, corner_ref, top_ref, out_ref):
    high, wide = mask_ref.shape
    col_even = lax.axis_index("col") % 2 == 0
    second = high + MAIN
    lane = lax.broadcasted_iota(jnp.int32, (high, wide), 1)

    def sides(a, b):
        return jnp.where(col_even, b, a), jnp.where(col_even, a, b)

    beside = [sides(edge1_ref[g * high : (g + 1) * high], edge2_ref[g * high : (g + 1) * high]) for g in range(2)]
    above = sides(corner_ref[:high], corner_ref[high:])
    below = sides(low_ref[:high], low_ref[second:])

    def edge(pair, w, at):
        left, right = pair
        if w == 0:
            return jnp.zeros_like(left)
        return jnp.where(lane < wide // 2, pltpu.roll(right, (wide - at) % wide, 1), pltpu.roll(left, (2 * wide - w - at) % wide, 1))

    def extended(i, own, rim):
        w, at = WIDTHS[i], ROW_AT[i]
        room = max(rim - at - w, 0)
        main = [jnp.zeros((room, wide), jnp.float32)] if room else []
        main += [top_ref[at + w - rim + room : at + w, :], own, low_ref[high + at : high + at + rim, :]]
        rest = [
            edge(above, CORNERS[i], CORNER_AT[i])[high - rim :],
            edge(beside[0 if i < PLANES else 1], w, LANE_AT[i]),
            edge(below, CORNERS[i], CORNER_AT[i])[:rim],
        ]
        return jnp.concatenate([jnp.concatenate(main, axis=0), jnp.concatenate(rest, axis=0)], axis=1)

    before = lambda v, axis: pltpu.roll(v, 1, axis)
    after = lambda v, axis: pltpu.roll(v, v.shape[axis] - 1, axis)
    rim = high
    height = extended(PLANES, state_ref[0], rim)
    zonal = extended(PLANES + 1, state_ref[1], rim)
    merid = extended(PLANES + 2, state_ref[2], rim)
    ocean = extended(PLANES + 3, mask_ref[...].astype(jnp.float32), rim)
    for s in range(SUB):
        reach = -(-2 * (SUB - s) // 8) * 8
        if reach < rim:
            cut = rim - reach
            height, zonal, merid, ocean = (v[cut : v.shape[0] - cut] for v in (height, zonal, merid, ocean))
            rim = reach
        push_u, push_v, push_h = (extended(s * DYN + f, force_ref[s * DYN + f], rim) for f in range(DYN))
        grad_x = (after(height, 0) - before(height, 0)) * 0.5
        grad_y = (after(height, 1) - before(height, 1)) * 0.5
        zonal = ocean * (zonal - grad_x + 0.2 * merid + 0.5 * push_u)
        merid = ocean * (merid - grad_y - 0.2 * zonal + 0.5 * push_v)
        spread = (after(zonal, 0) - before(zonal, 0)) * 0.5 + (after(merid, 1) - before(merid, 1)) * 0.5
        height = height - spread + 0.5 * push_h
    for k, value in enumerate((height, zonal, merid)):
        out_ref[k] = value[rim : rim + high, :wide]


def per_device(size_row, size_col, atmo_states, remap_weights, intersection_tiles, land_mask, ocean_state):
    fields, levels, tiles, cells = atmo_states.shape
    high, wide = land_mask.shape
    rows = PLANES + fields - DYN
    vmem = pl.BlockSpec(memory_space=pltpu.VMEM)
    f32 = lambda *shape: jax.ShapeDtypeStruct(shape, jnp.float32)
    params = lambda: pltpu.CompilerParams(vmem_limit_bytes=32 << 20)

    onward = [(i, (i + 1) % size_row) for i in range(size_row)]
    back = [(j, i) for i, j in onward]
    col_near = [(i, i ^ 1) for i in range(size_col)]
    col_far = [(i, (i + 1) % size_col if i % 2 else (i - 1) % size_col) for i in range(size_col)]
    half = tiles // 2
    names = intersection_tiles.T

    table = hermite_table(SUB, levels).astype(np.float32)
    mean = table.astype(np.float64).mean(axis=0)
    own, part = pl.pallas_call(
        functools.partial(interp_kernel, table, mean, rows),
        out_shape=(f32(tiles * rows, cells), f32(half * rows, cells)),
        in_specs=[vmem],
        out_specs=(vmem, vmem),
        compiler_params=params(),
        cost_estimate=pl.CostEstimate(flops=10**10, bytes_accessed=4 << 20, transcendentals=0),
    )(atmo_states)
    previous = lax.ppermute(part, "row", onward)
    following = lax.ppermute(part, "row", back)

    acc, rest = pl.pallas_call(
        functools.partial(own_kernel, rows),
        out_shape=(f32(32, high, wide), jax.ShapeDtypeStruct((high, 2 * cells, 2 * wide), jnp.bfloat16)),
        in_specs=[vmem] * 3,
        out_specs=(vmem, vmem),
        scratch_shapes=[pltpu.VMEM((tiles, 64, cells), jnp.bfloat16)],
        compiler_params=params(),
        cost_estimate=pl.CostEstimate(flops=10**9, bytes_accessed=4 << 20, transcendentals=0),
    )(names, own, remap_weights)

    following, previous, acc, rest = lax.optimization_barrier((following, previous, acc, rest))
    near = jnp.stack([previous, following])
    far = lax.ppermute(near, "col", col_near)

    total, down, up, edge1, edge2 = pl.pallas_call(
        functools.partial(rim_kernel, rows),
        out_shape=(f32(32, high, wide), f32(MAIN, wide), f32(MAIN, wide), f32(GROUPS * high, wide), f32(GROUPS * high, wide)),
        in_specs=[vmem] * 7,
        out_specs=(vmem,) * 5,
        scratch_shapes=[pltpu.VMEM((2 * tiles, 64, cells), jnp.bfloat16)],
        compiler_params=params(),
        cost_estimate=pl.CostEstimate(flops=10**9, bytes_accessed=4 << 20, transcendentals=0),
    )(names, near, far, rest, acc, ocean_state, land_mask)
    forced = total[:PLANES].reshape(SUB, DYN, high, wide)
    flux_mean = jnp.concatenate([jnp.mean(forced, axis=0), total[PLANES:rows]], axis=0)

    from1 = lax.ppermute(edge1, "col", col_near)
    from2 = lax.ppermute(edge2, "col", col_far)
    from2, from1 = lax.optimization_barrier((from2, from1))
    corners = from1[2 * high :], from2[2 * high :]
    top = lax.ppermute(down, "row", onward)
    corner = lax.ppermute(jnp.concatenate(corners), "row", onward)
    low = lax.ppermute(jnp.concatenate([corners[0], up, corners[1]]), "row", back)

    final = pl.pallas_call(
        ocean_kernel,
        out_shape=f32(3, high, wide),
        in_specs=[vmem] * 8,
        out_specs=vmem,
        compiler_params=params(),
    )(total, ocean_state, land_mask, from1, from2, low, corner, top)
    return flux_mean, final


def solution(mesh):
    placed = (
        P(None, None, "row", None),
        P("row", "col", None, None),
        P("row", "col"),
        P("row", "col"),
        P(None, "row", "col"),
    )
    return jax.shard_map(
        functools.partial(per_device, mesh.shape["row"], mesh.shape["col"]),
        mesh=mesh,
        in_specs=placed,
        out_specs=(P(None, "row", "col"), P(None, "row", "col")),
        check_vma=False,
    )
```

```python
import functools
import math

import jax
import jax.numpy as jnp
import numpy as np
from jax import lax
from jax.experimental import pallas as pl
from jax.experimental.pallas import tpu as pltpu
from jax.sharding import PartitionSpec as P

SUB = 6
DYN = 3


def hermite_table(count_sub, count_levels):
    table = np.zeros((count_sub, count_levels))

    def add_slope(position_row, level, factor):
        if level == 0:
            table[position_row, 1] += factor
            table[position_row, 0] -= factor
        elif level == count_levels - 1:
            table[position_row, level] += factor
            table[position_row, level - 1] -= factor
        else:
            table[position_row, level + 1] += 0.5 * factor
            table[position_row, level - 1] -= 0.5 * factor

    for substep in range(count_sub):
        position = (substep + 0.5) * (count_levels - 1) / count_sub
        lower = min(int(math.floor(position)), count_levels - 2)
        fraction = position - lower
        table[substep, lower] += 2 * fraction**3 - 3 * fraction**2 + 1
        table[substep, lower + 1] += -2 * fraction**3 + 3 * fraction**2
        add_slope(substep, lower, fraction**3 - 2 * fraction**2 + fraction)
        add_slope(substep, lower + 1, fraction**3 - fraction**2)
    return table


WIDTHS = [2 * (SUB - s) - (1 if f < 2 else 2) for s in range(SUB) for f in range(DYN)]
WIDTHS += [2 * SUB, 2 * SUB - 1, 2 * SUB - 1, 2 * SUB - 1]
PLANES = SUB * DYN
ITEMS = len(WIDTHS)
ROW_AT = np.concatenate([[0], np.cumsum(WIDTHS)]).tolist()
LANE_AT = ROW_AT[:PLANES] + [ROW_AT[i] - ROW_AT[PLANES] for i in range(PLANES, ITEMS)]
CORNERS = [max(w - 1, 0) for w in WIDTHS]
CORNER_AT = np.concatenate([[0], np.cumsum(CORNERS)]).tolist()
MAIN = -(-ROW_AT[-1] // 8) * 8
GROUPS = 3


def interp_kernel(table, mean, rows, atmo_ref, out_ref, half_ref):
    fields, levels, tiles, _ = atmo_ref.shape
    for f in range(fields):
        level = [atmo_ref[f, k] for k in range(levels)]
        if f < DYN:
            for s in range(SUB):
                terms = [float(table[s, k]) * level[k] for k in range(levels) if table[s, k] != 0]
                out_ref[pl.ds(s * DYN + f, tiles, stride=rows), :] = functools.reduce(jnp.add, terms)
        else:
            terms = [float(mean[k]) * level[k] for k in range(levels)]
            out_ref[pl.ds(PLANES + f - DYN, tiles, stride=rows), :] = functools.reduce(jnp.add, terms)
    part = half_ref.shape[0]
    half_ref[...] = out_ref[pl.ds(pl.multiple_of(lax.axis_index("col") % 2 * part, 8), part), :]


def split_tiles(source_ref, split_ref, base, rows):
    tiles = source_ref.shape[0] // rows
    for g in range(tiles):
        value = source_ref[g * rows : min(g * rows + 32, source_ref.shape[0]), :]
        if value.shape[0] < 32:
            value = jnp.concatenate([value, jnp.zeros((32 - value.shape[0], value.shape[1]), value.dtype)], axis=0)
        high = value.astype(jnp.bfloat16)
        split_ref[base + g, 0:32, :] = high
        split_ref[base + g, 32:64, :] = (value - high.astype(jnp.float32)).astype(jnp.bfloat16)


def split_weights(wa, wb):
    weights = jnp.concatenate([wa, wb], axis=0)
    high = weights.astype(jnp.bfloat16)
    low = (weights - high.astype(jnp.float32)).astype(jnp.bfloat16)
    return jnp.concatenate([high, low], axis=1)


def remap_row(left, weights):
    both = jnp.dot(left, weights, preferred_element_type=jnp.float32)
    wide = weights.shape[1] // 2
    return both[0:32, :wide] + both[32:64, :wide] + both[0:32, wide:]


def own_kernel(rows, tiles_ref, own_ref, weight_ref, acc_ref, rest_ref, split_ref):
    index = tiles_ref[...] - split_ref.shape[0]
    split_tiles(own_ref, split_ref, 0, rows)
    for x in range(weight_ref.shape[0]):
        first, second = index[1, x], index[2, x]
        weights = split_weights(weight_ref[x, 1], weight_ref[x, 2])
        acc_ref[:, x, :] = remap_row(jnp.concatenate([split_ref[first], split_ref[second]], axis=1), weights)
        rest_ref[x] = split_weights(weight_ref[x, 0], weight_ref[x, 3])


def add_slot(rows, slot, offset, tiles_ref, near_ref, far_ref, rest_ref, add_ref, total_ref, split_ref):
    part = split_ref.shape[0] // 2
    split_tiles(near_ref, split_ref, 0, rows)
    split_tiles(far_ref, split_ref, part, rows)
    col_odd = lax.axis_index("col") % 2
    name = tiles_ref[...] - offset * 2 * part
    index = name % part + part * ((name // part + col_odd) % 2)
    cells = split_ref.shape[2]
    at = (slot > 0) * cells
    for x in range(rest_ref.shape[0]):
        total_ref[:, x, :] = remap_row(split_ref[index[slot, x]], rest_ref[x, at : at + cells, :]) + add_ref[:, x, :]


def rim_kernel(rows, tiles_ref, near_ref, far_ref, rest_ref, add_ref, state_ref, mask_ref,
               total_ref, down_ref, up_ref, edge1_ref, edge2_ref, split_ref):
    add_slot(rows, 3, 2, tiles_ref, near_ref, far_ref, rest_ref, add_ref, total_ref, split_ref)
    col_odd = lax.axis_index("col") % 2

    items = [total_ref[p] for p in range(PLANES)] + [state_ref[k] for k in range(DYN)] + [mask_ref[...].astype(jnp.float32)]
    high, wide = mask_ref.shape
    col_even = col_odd == 0

    for i, value in enumerate(items):
        w, at = WIDTHS[i], ROW_AT[i]
        if w:
            down_ref[at : at + w, :] = value[high - w :]
            up_ref[at : at + w, :] = value[:w]
    for ref in (down_ref, up_ref):
        ref[ROW_AT[-1] :, :] = jnp.zeros((MAIN - ROW_AT[-1], wide), jnp.float32)

    lane = lax.broadcasted_iota(jnp.int32, (high, wide), 1)
    groups = ((range(PLANES), WIDTHS, LANE_AT), (range(PLANES, ITEMS), WIDTHS, LANE_AT), (range(ITEMS), CORNERS, CORNER_AT))
    for g, (members, widths, places) in enumerate(groups):
        last = jnp.zeros((high, wide), jnp.float32)
        head = jnp.zeros((high, wide), jnp.float32)
        for i in members:
            w, at = widths[i], places[i]
            if w:
                last = jnp.where(lane >= at, pltpu.roll(items[i], (at + w) % wide, 1), last)
                head = jnp.where(lane >= at, pltpu.roll(items[i], at, 1), head)
        edge1_ref[g * high : (g + 1) * high, :] = jnp.where(col_even, last, head)
        edge2_ref[g * high : (g + 1) * high, :] = jnp.where(col_even, head, last)


def ocean_kernel(force_ref, state_ref, mask_ref, edge1_ref, edge2_ref, low_ref, corner_ref, top_ref, out_ref, *shift_refs):
    high, wide = mask_ref.shape
    col_even = lax.axis_index("col") % 2 == 0
    second = high + MAIN
    lane = lax.broadcasted_iota(jnp.int32, (high, wide), 1)

    def sides(a, b):
        return jnp.where(col_even, b, a), jnp.where(col_even, a, b)

    beside = [sides(edge1_ref[g * high : (g + 1) * high], edge2_ref[g * high : (g + 1) * high]) for g in range(2)]
    above = sides(corner_ref[:high], corner_ref[high:])
    below = sides(low_ref[:high], low_ref[second:])

    def edge(pair, w, at):
        left, right = pair
        if w == 0:
            return jnp.zeros_like(left)
        return jnp.where(lane < wide // 2, pltpu.roll(right, (wide - at) % wide, 1), pltpu.roll(left, (2 * wide - w - at) % wide, 1))

    def extended(i, own, rim):
        w, at = WIDTHS[i], ROW_AT[i]
        room = max(rim - at - w, 0)
        main = [jnp.zeros((room, wide), jnp.float32)] if room else []
        main += [top_ref[at + w - rim + room : at + w, :], own, low_ref[high + at : high + at + rim, :]]
        rest = [
            edge(above, CORNERS[i], CORNER_AT[i])[high - rim :],
            edge(beside[0 if i < PLANES else 1], w, LANE_AT[i]),
            edge(below, CORNERS[i], CORNER_AT[i])[:rim],
        ]
        return [jnp.concatenate(main, axis=0), jnp.concatenate(rest, axis=0)]

    each = lambda f, *fields: [f(*parts) for parts in zip(*fields)]

    def slope_x(field, refs):
        out = []
        for ref, value in zip(refs, field):
            rows = value.shape[0]
            ref[8 : 8 + rows, :] = value
            out.append((ref[9 : 9 + rows, :] - ref[7 : 7 + rows, :]) * 0.5)
        return out

    def along(field, step):
        place = lax.broadcasted_iota(jnp.int32, field[0].shape, 1)
        crosses = place >= wide - step if step > 0 else place < -step
        moved = [pltpu.roll(v, -step % wide, 1) for v in field]
        return [jnp.where(crosses, moved[1], moved[0]), jnp.where(crosses, moved[0], moved[1])]

    def slope_y(field):
        return each(lambda a, b: (a - b) * 0.5, along(field, 1), along(field, -1))

    def slope_yy(field):
        return each(lambda a, v, b: ((a - v) - (v - b)) * 0.25, along(field, 2), field, along(field, -2))

    rim = high
    height = extended(PLANES, state_ref[0], rim)
    zonal = extended(PLANES + 1, state_ref[1], rim)
    merid = extended(PLANES + 2, state_ref[2], rim)
    ocean = extended(PLANES + 3, mask_ref[...].astype(jnp.float32), rim)
    grad_y = slope_y(height)
    for s in range(SUB):
        reach = -(-2 * (SUB - s) // 8) * 8
        if reach < rim:
            cut = rim - reach
            height, zonal, merid, ocean, grad_y = (
                each(lambda v: v[cut : v.shape[0] - cut], field) for field in (height, zonal, merid, ocean, grad_y)
            )
            rim = reach
        push_u, push_v, push_h = (extended(s * DYN + f, force_ref[s * DYN + f], rim) for f in range(DYN))
        grad_x = slope_x(height, shift_refs[:2])
        zonal = each(lambda m, u, g, v, p: m * (u - g + 0.2 * v + 0.5 * p), ocean, zonal, grad_x, merid, push_u)
        merid = each(lambda m, v, g, u, p: m * (v - g - 0.2 * u + 0.5 * p), ocean, merid, grad_y, zonal, push_v)
        spread = each(jnp.add, slope_x(zonal, shift_refs[2:]), slope_y(merid))
        height = each(lambda h, d, p: h - d + 0.5 * p, height, spread, push_h)
        if s < SUB - 1:
            bend = each(jnp.add, slope_x(slope_y(zonal), shift_refs[4:]), slope_yy(merid))
            grad_y = each(lambda g, d, p: g - d + 0.5 * p, grad_y, bend, slope_y(push_h))
    for k, value in enumerate((height, zonal, merid)):
        out_ref[k] = value[0][rim : rim + high]


def per_device(size_row, size_col, atmo_states, remap_weights, intersection_tiles, land_mask, ocean_state):
    fields, levels, tiles, cells = atmo_states.shape
    high, wide = land_mask.shape
    rows = PLANES + fields - DYN
    vmem = pl.BlockSpec(memory_space=pltpu.VMEM)
    f32 = lambda *shape: jax.ShapeDtypeStruct(shape, jnp.float32)
    params = lambda: pltpu.CompilerParams(vmem_limit_bytes=32 << 20)

    onward = [(i, (i + 1) % size_row) for i in range(size_row)]
    back = [(j, i) for i, j in onward]
    col_near = [(i, i ^ 1) for i in range(size_col)]
    col_far = [(i, (i + 1) % size_col if i % 2 else (i - 1) % size_col) for i in range(size_col)]
    half = tiles // 2
    names = intersection_tiles.T

    table = hermite_table(SUB, levels).astype(np.float32)
    mean = table.astype(np.float64).mean(axis=0)
    own, part = pl.pallas_call(
        functools.partial(interp_kernel, table, mean, rows),
        out_shape=(f32(tiles * rows, cells), f32(half * rows, cells)),
        in_specs=[vmem],
        out_specs=(vmem, vmem),
        compiler_params=params(),
        cost_estimate=pl.CostEstimate(flops=10**10, bytes_accessed=4 << 20, transcendentals=0),
    )(atmo_states)
    previous = lax.ppermute(part, "row", onward)
    following = lax.ppermute(part, "row", back)

    acc, rest = pl.pallas_call(
        functools.partial(own_kernel, rows),
        out_shape=(f32(32, high, wide), jax.ShapeDtypeStruct((high, 2 * cells, 2 * wide), jnp.bfloat16)),
        in_specs=[vmem] * 3,
        out_specs=(vmem, vmem),
        scratch_shapes=[pltpu.VMEM((tiles, 64, cells), jnp.bfloat16)],
        compiler_params=params(),
        cost_estimate=pl.CostEstimate(flops=10**9, bytes_accessed=4 << 20, transcendentals=0),
    )(names, own, remap_weights)

    previous, acc, rest = lax.optimization_barrier((previous, acc, rest))
    previous_far = lax.ppermute(previous, "col", col_near)
    following_far = lax.ppermute(following, "col", col_near)
    acc = pl.pallas_call(
        functools.partial(add_slot, rows, 0, 0),
        out_shape=f32(32, high, wide),
        in_specs=[vmem] * 5,
        out_specs=vmem,
        scratch_shapes=[pltpu.VMEM((tiles, 64, cells), jnp.bfloat16)],
        compiler_params=params(),
        cost_estimate=pl.CostEstimate(flops=10**9, bytes_accessed=2 << 20, transcendentals=0),
    )(names, previous, previous_far, rest, acc)

    total, down, up, edge1, edge2 = pl.pallas_call(
        functools.partial(rim_kernel, rows),
        out_shape=(f32(32, high, wide), f32(MAIN, wide), f32(MAIN, wide), f32(GROUPS * high, wide), f32(GROUPS * high, wide)),
        in_specs=[vmem] * 7,
        out_specs=(vmem,) * 5,
        scratch_shapes=[pltpu.VMEM((tiles, 64, cells), jnp.bfloat16)],
        compiler_params=params(),
        cost_estimate=pl.CostEstimate(flops=10**9, bytes_accessed=4 << 20, transcendentals=0),
    )(names, following, following_far, rest, acc, ocean_state, land_mask)
    forced = total[:PLANES].reshape(SUB, DYN, high, wide)
    flux_mean = jnp.concatenate([jnp.mean(forced, axis=0), total[PLANES:rows]], axis=0)

    from1 = lax.ppermute(edge1, "col", col_near)
    from2 = lax.ppermute(edge2, "col", col_far)
    from2, from1 = lax.optimization_barrier((from2, from1))
    corners = from1[2 * high :], from2[2 * high :]
    top = lax.ppermute(down, "row", onward)
    corner = lax.ppermute(jnp.concatenate(corners), "row", onward)
    low = lax.ppermute(jnp.concatenate([corners[0], up, corners[1]]), "row", back)

    final = pl.pallas_call(
        ocean_kernel,
        out_shape=f32(3, high, wide),
        in_specs=[vmem] * 8,
        out_specs=vmem,
        scratch_shapes=[pltpu.VMEM((3 * high + 16, wide), jnp.float32)] * 6,
        compiler_params=params(),
    )(total, ocean_state, land_mask, from1, from2, low, corner, top)
    return flux_mean, final


def solution(mesh):
    placed = (
        P(None, None, "row", None),
        P("row", "col", None, None),
        P("row", "col"),
        P("row", "col"),
        P(None, "row", "col"),
    )
    return jax.shard_map(
        functools.partial(per_device, mesh.shape["row"], mesh.shape["col"]),
        mesh=mesh,
        in_specs=placed,
        out_specs=(P(None, "row", "col"), P(None, "row", "col")),
        check_vma=False,
    )
```

```python
import functools
import math

import jax
import jax.numpy as jnp
import numpy as np
from jax import lax
from jax.experimental import pallas as pl
from jax.experimental.pallas import tpu as pltpu
from jax.sharding import PartitionSpec as P

SUB = 6
DYN = 3


def hermite_table(count_sub, count_levels):
    table = np.zeros((count_sub, count_levels))

    def add_slope(position_row, level, factor):
        if level == 0:
            table[position_row, 1] += factor
            table[position_row, 0] -= factor
        elif level == count_levels - 1:
            table[position_row, level] += factor
            table[position_row, level - 1] -= factor
        else:
            table[position_row, level + 1] += 0.5 * factor
            table[position_row, level - 1] -= 0.5 * factor

    for substep in range(count_sub):
        position = (substep + 0.5) * (count_levels - 1) / count_sub
        lower = min(int(math.floor(position)), count_levels - 2)
        fraction = position - lower
        table[substep, lower] += 2 * fraction**3 - 3 * fraction**2 + 1
        table[substep, lower + 1] += -2 * fraction**3 + 3 * fraction**2
        add_slope(substep, lower, fraction**3 - 2 * fraction**2 + fraction)
        add_slope(substep, lower + 1, fraction**3 - fraction**2)
    return table


WIDTHS = [2 * (SUB - s) - (1 if f < 2 else 2) for s in range(SUB) for f in range(DYN)]
WIDTHS += [2 * SUB, 2 * SUB - 1, 2 * SUB - 1, 2 * SUB - 1]
PLANES = SUB * DYN
ITEMS = len(WIDTHS)
ROW_AT = np.concatenate([[0], np.cumsum(WIDTHS)]).tolist()
LANE_AT = ROW_AT[:PLANES] + [ROW_AT[PLANES] + i for i in range(ITEMS - PLANES)]
CORNERS = [max(w - 1, 0) for w in WIDTHS]
CORNER_AT = np.concatenate([[0], np.cumsum(CORNERS)]).tolist()
MAIN = -(-ROW_AT[-1] // 8) * 8
GROUPS = 2


def interp_kernel(table, mean, rows, first_ref, second_ref, out_ref, half_ref):
    part, levels, tiles, _ = first_ref.shape
    fields = part + second_ref.shape[0]
    for f in range(fields):
        level = [first_ref[f, k] if f < part else second_ref[f - part, k] for k in range(levels)]
        if f < DYN:
            for s in range(SUB):
                terms = [float(table[s, k]) * level[k] for k in range(levels) if table[s, k] != 0]
                out_ref[pl.ds(s * DYN + f, tiles, stride=rows), :] = functools.reduce(jnp.add, terms)
        else:
            terms = [float(mean[k]) * level[k] for k in range(levels)]
            out_ref[pl.ds(PLANES + f - DYN, tiles, stride=rows), :] = functools.reduce(jnp.add, terms)
    size = half_ref.shape[0]
    half_ref[...] = out_ref[pl.ds(pl.multiple_of(lax.axis_index("col") % 2 * size, 8), size), :]


def split_tiles(source_ref, split_ref, base, rows):
    tiles = source_ref.shape[0] // rows
    for g in range(tiles):
        value = source_ref[g * rows : min(g * rows + 32, source_ref.shape[0]), :]
        if value.shape[0] < 32:
            value = jnp.concatenate([value, jnp.zeros((32 - value.shape[0], value.shape[1]), value.dtype)], axis=0)
        high = value.astype(jnp.bfloat16)
        split_ref[base + g, 0:32, :] = high
        split_ref[base + g, 32:64, :] = (value - high.astype(jnp.float32)).astype(jnp.bfloat16)


def split_weights(wa, wb):
    weights = jnp.concatenate([wa, wb], axis=0)
    high = weights.astype(jnp.bfloat16)
    low = (weights - high.astype(jnp.float32)).astype(jnp.bfloat16)
    return jnp.concatenate([high, low], axis=1)


def remap_row(left, weights):
    both = jnp.dot(left, weights, preferred_element_type=jnp.float32)
    wide = weights.shape[1] // 2
    return both[0:32, :wide] + both[32:64, :wide] + both[0:32, wide:]


def own_kernel(rows, tiles_ref, own_ref, weight_ref, acc_ref, rest_ref, split_ref):
    index = tiles_ref[...] - split_ref.shape[0]
    split_tiles(own_ref, split_ref, 0, rows)
    for x in range(weight_ref.shape[0]):
        first, second = index[1, x], index[2, x]
        weights = split_weights(weight_ref[x, 1], weight_ref[x, 2])
        acc_ref[:, x, :] = remap_row(jnp.concatenate([split_ref[first], split_ref[second]], axis=1), weights)
        rest_ref[x] = split_weights(weight_ref[x, 0], weight_ref[x, 3])


def add_slot(rows, slot, offset, tiles_ref, near_ref, far_ref, rest_ref, add_ref, total_ref, split_ref):
    part = split_ref.shape[0] // 2
    split_tiles(near_ref, split_ref, 0, rows)
    split_tiles(far_ref, split_ref, part, rows)
    col_odd = lax.axis_index("col") % 2
    name = tiles_ref[...] - offset * 2 * part
    index = name % part + part * ((name // part + col_odd) % 2)
    cells = split_ref.shape[2]
    at = (slot > 0) * cells
    for x in range(rest_ref.shape[0]):
        total_ref[:, x, :] = remap_row(split_ref[index[slot, x]], rest_ref[x, at : at + cells, :]) + add_ref[:, x, :]


def rim_kernel(rows, tiles_ref, near_ref, far_ref, rest_ref, add_ref, state_ref, mask_ref,
               total_ref, down_ref, up_ref, edge1_ref, edge2_ref, split_ref):
    add_slot(rows, 3, 2, tiles_ref, near_ref, far_ref, rest_ref, add_ref, total_ref, split_ref)
    col_odd = lax.axis_index("col") % 2

    items = [total_ref[p] for p in range(PLANES)] + [state_ref[k] for k in range(DYN)] + [mask_ref[...].astype(jnp.float32)]
    high, wide = mask_ref.shape
    col_even = col_odd == 0

    for i, value in enumerate(items):
        w, at = WIDTHS[i], ROW_AT[i]
        if w:
            down_ref[at : at + w, :] = value[high - w :]
            up_ref[at : at + w, :] = value[:w]
    for ref in (down_ref, up_ref):
        ref[ROW_AT[-1] :, :] = jnp.zeros((MAIN - ROW_AT[-1], wide), jnp.float32)

    lane = lax.broadcasted_iota(jnp.int32, (high, wide), 1)
    own = [(i, WIDTHS[i] if i < PLANES else 1, WIDTHS[i], LANE_AT[i]) for i in range(ITEMS)]
    out = [(i, CORNERS[i], CORNERS[i], CORNER_AT[i]) for i in range(ITEMS)]
    for g, group in enumerate((own, out)):
        last = jnp.zeros((high, wide), jnp.float32)
        head = jnp.zeros((high, wide), jnp.float32)
        for i, count, w, at in group:
            if count:
                last = jnp.where(lane >= at, pltpu.roll(items[i], (at + w) % wide, 1), last)
                head = jnp.where(lane >= at, pltpu.roll(items[i], (at + count - w) % wide, 1), head)
        edge1_ref[g * high : (g + 1) * high, :] = jnp.where(col_even, last, head)
        edge2_ref[g * high : (g + 1) * high, :] = jnp.where(col_even, head, last)


def ocean_kernel(force_ref, state_ref, mask_ref, edge1_ref, edge2_ref, low_ref, corner_ref, top_ref, out_ref, *shift_refs):
    high, wide = mask_ref.shape
    col_even = lax.axis_index("col") % 2 == 0
    second = high + MAIN
    lane = lax.broadcasted_iota(jnp.int32, (high, wide), 1)

    def sides(a, b):
        return jnp.where(col_even, b, a), jnp.where(col_even, a, b)

    beside = [sides(edge1_ref[g * high : (g + 1) * high], edge2_ref[g * high : (g + 1) * high]) for g in range(2)]
    above = sides(corner_ref[:high], corner_ref[high:])
    below = sides(low_ref[:high], low_ref[second:])

    def edge(pair, w, at):
        left, right = pair
        if w == 0:
            return jnp.zeros_like(left)
        return jnp.where(lane < wide // 2, pltpu.roll(right, (wide - at) % wide, 1), pltpu.roll(left, (2 * wide - w - at) % wide, 1))

    def extended(i, own, rim):
        w, at = WIDTHS[i], ROW_AT[i]
        room = max(rim - at - w, 0)
        main = [jnp.zeros((room, wide), jnp.float32)] if room else []
        main += [top_ref[at + w - rim + room : at + w, :], own, low_ref[high + at : high + at + rim, :]]
        if i < PLANES:
            along_own = edge(beside[0], w, LANE_AT[i])
        else:
            along_own = edge(beside[1], CORNERS[i], CORNER_AT[i])
            left, right = beside[0]
            along_own = jnp.where(lane == w - 1, pltpu.roll(right, (wide + w - 1 - LANE_AT[i]) % wide, 1), along_own)
            along_own = jnp.where(lane == wide - w, pltpu.roll(left, (2 * wide - w - LANE_AT[i]) % wide, 1), along_own)
        rest = [
            edge(above, CORNERS[i], CORNER_AT[i])[high - rim :],
            along_own,
            edge(below, CORNERS[i], CORNER_AT[i])[:rim],
        ]
        return [jnp.concatenate(main, axis=0), jnp.concatenate(rest, axis=0)]

    each = lambda f, *fields: [f(*parts) for parts in zip(*fields)]

    def slope_x(field, refs):
        out = []
        for ref, value in zip(refs, field):
            rows = value.shape[0]
            ref[8 : 8 + rows, :] = value
            out.append((ref[9 : 9 + rows, :] - ref[7 : 7 + rows, :]) * 0.5)
        return out

    def along(field, step):
        place = lax.broadcasted_iota(jnp.int32, field[0].shape, 1)
        crosses = place >= wide - step if step > 0 else place < -step
        moved = [pltpu.roll(v, -step % wide, 1) for v in field]
        return [jnp.where(crosses, moved[1], moved[0]), jnp.where(crosses, moved[0], moved[1])]

    def slope_y(field):
        return each(lambda a, b: (a - b) * 0.5, along(field, 1), along(field, -1))

    def slope_yy(field):
        return each(lambda a, v, b: ((a - v) - (v - b)) * 0.25, along(field, 2), field, along(field, -2))

    rim = high
    height = extended(PLANES, state_ref[0], rim)
    zonal = extended(PLANES + 1, state_ref[1], rim)
    merid = extended(PLANES + 2, state_ref[2], rim)
    ocean = extended(PLANES + 3, mask_ref[...].astype(jnp.float32), rim)
    grad_y = slope_y(height)
    for s in range(SUB):
        reach = -(-2 * (SUB - s) // 8) * 8
        if reach < rim:
            cut = rim - reach
            height, zonal, merid, ocean, grad_y = (
                each(lambda v: v[cut : v.shape[0] - cut], field) for field in (height, zonal, merid, ocean, grad_y)
            )
            rim = reach
        push_u, push_v, push_h = (extended(s * DYN + f, force_ref[s * DYN + f], rim) for f in range(DYN))
        grad_x = slope_x(height, shift_refs[:2])
        zonal = each(lambda m, u, g, v, p: m * (u - g + 0.2 * v + 0.5 * p), ocean, zonal, grad_x, merid, push_u)
        merid = each(lambda m, v, g, u, p: m * (v - g - 0.2 * u + 0.5 * p), ocean, merid, grad_y, zonal, push_v)
        slope = slope_x(zonal, shift_refs[2:])
        spread = each(jnp.add, slope, slope_y(merid))
        height = each(lambda h, d, p: h - d + 0.5 * p, height, spread, push_h)
        if s < SUB - 1:
            rest = slope_y(each(lambda d, p: 0.5 * p - d, slope, push_h))
            grad_y = each(lambda g, r, b: g + r - b, grad_y, rest, slope_yy(merid))
    for k, value in enumerate((height, zonal, merid)):
        out_ref[k] = value[0][rim : rim + high]


def per_device(size_row, size_col, atmo_states, remap_weights, intersection_tiles, land_mask, ocean_state):
    fields, levels, tiles, cells = atmo_states.shape
    high, wide = land_mask.shape
    rows = PLANES + fields - DYN
    vmem = pl.BlockSpec(memory_space=pltpu.VMEM)
    f32 = lambda *shape: jax.ShapeDtypeStruct(shape, jnp.float32)
    params = lambda: pltpu.CompilerParams(vmem_limit_bytes=32 << 20)

    onward = [(i, (i + 1) % size_row) for i in range(size_row)]
    back = [(j, i) for i, j in onward]
    col_near = [(i, i ^ 1) for i in range(size_col)]
    col_far = [(i, (i + 1) % size_col if i % 2 else (i - 1) % size_col) for i in range(size_col)]
    half = tiles // 2
    names = intersection_tiles.T

    table = hermite_table(SUB, levels).astype(np.float32)
    mean = table.astype(np.float64).mean(axis=0)
    own, part = pl.pallas_call(
        functools.partial(interp_kernel, table, mean, rows),
        out_shape=(f32(tiles * rows, cells), f32(half * rows, cells)),
        in_specs=[vmem] * 2,
        out_specs=(vmem, vmem),
        compiler_params=params(),
        cost_estimate=pl.CostEstimate(flops=10**10, bytes_accessed=4 << 20, transcendentals=0),
    )(atmo_states[: fields // 2], atmo_states[fields // 2 :])
    previous = lax.ppermute(part, "row", onward)
    following = lax.ppermute(part, "row", back)

    acc, rest = pl.pallas_call(
        functools.partial(own_kernel, rows),
        out_shape=(f32(32, high, wide), jax.ShapeDtypeStruct((high, 2 * cells, 2 * wide), jnp.bfloat16)),
        in_specs=[vmem] * 3,
        out_specs=(vmem, vmem),
        scratch_shapes=[pltpu.VMEM((tiles, 64, cells), jnp.bfloat16)],
        compiler_params=params(),
        cost_estimate=pl.CostEstimate(flops=10**9, bytes_accessed=4 << 20, transcendentals=0),
    )(names, own, remap_weights)

    previous, acc, rest = lax.optimization_barrier((previous, acc, rest))
    previous_far = lax.ppermute(previous, "col", col_near)
    following_far = lax.ppermute(following, "col", col_near)
    acc = pl.pallas_call(
        functools.partial(add_slot, rows, 0, 0),
        out_shape=f32(32, high, wide),
        in_specs=[vmem] * 5,
        out_specs=vmem,
        scratch_shapes=[pltpu.VMEM((tiles, 64, cells), jnp.bfloat16)],
        compiler_params=params(),
        cost_estimate=pl.CostEstimate(flops=10**9, bytes_accessed=2 << 20, transcendentals=0),
    )(names, previous, previous_far, rest, acc)

    total, down, up, edge1, edge2 = pl.pallas_call(
        functools.partial(rim_kernel, rows),
        out_shape=(f32(32, high, wide), f32(MAIN, wide), f32(MAIN, wide), f32(GROUPS * high, wide), f32(GROUPS * high, wide)),
        in_specs=[vmem] * 7,
        out_specs=(vmem,) * 5,
        scratch_shapes=[pltpu.VMEM((tiles, 64, cells), jnp.bfloat16)],
        compiler_params=params(),
        cost_estimate=pl.CostEstimate(flops=10**9, bytes_accessed=4 << 20, transcendentals=0),
    )(names, following, following_far, rest, acc, ocean_state, land_mask)
    forced = total[:PLANES].reshape(SUB, DYN, high, wide)
    flux_mean = jnp.concatenate([jnp.mean(forced, axis=0), total[PLANES:rows]], axis=0)

    from1 = lax.ppermute(edge1, "col", col_near)
    from2 = lax.ppermute(edge2, "col", col_far)
    from2, from1 = lax.optimization_barrier((from2, from1))
    corners = from1[high:], from2[high:]
    top = lax.ppermute(down, "row", onward)
    corner = lax.ppermute(jnp.concatenate(corners), "row", onward)
    low = lax.ppermute(jnp.concatenate([corners[0], up, corners[1]]), "row", back)

    final = pl.pallas_call(
        ocean_kernel,
        out_shape=f32(3, high, wide),
        in_specs=[vmem] * 8,
        out_specs=vmem,
        scratch_shapes=[pltpu.VMEM((3 * high + 16, wide), jnp.float32)] * 4,
        compiler_params=params(),
    )(total, ocean_state, land_mask, from1, from2, low, corner, top)
    return flux_mean, final


def solution(mesh):
    placed = (
        P(None, None, "row", None),
        P("row", "col", None, None),
        P("row", "col"),
        P("row", "col"),
        P(None, "row", "col"),
    )
    return jax.shard_map(
        functools.partial(per_device, mesh.shape["row"], mesh.shape["col"]),
        mesh=mesh,
        in_specs=placed,
        out_specs=(P(None, "row", "col"), P(None, "row", "col")),
        check_vma=False,
    )
```

```python
import functools
import math

import jax
import jax.numpy as jnp
import numpy as np
from jax import lax
from jax.experimental import pallas as pl
from jax.experimental.pallas import tpu as pltpu
from jax.sharding import PartitionSpec as P

SUB = 6
DYN = 3


def hermite_table(count_sub, count_levels):
    table = np.zeros((count_sub, count_levels))

    def add_slope(position_row, level, factor):
        if level == 0:
            table[position_row, 1] += factor
            table[position_row, 0] -= factor
        elif level == count_levels - 1:
            table[position_row, level] += factor
            table[position_row, level - 1] -= factor
        else:
            table[position_row, level + 1] += 0.5 * factor
            table[position_row, level - 1] -= 0.5 * factor

    for substep in range(count_sub):
        position = (substep + 0.5) * (count_levels - 1) / count_sub
        lower = min(int(math.floor(position)), count_levels - 2)
        fraction = position - lower
        table[substep, lower] += 2 * fraction**3 - 3 * fraction**2 + 1
        table[substep, lower + 1] += -2 * fraction**3 + 3 * fraction**2
        add_slope(substep, lower, fraction**3 - 2 * fraction**2 + fraction)
        add_slope(substep, lower + 1, fraction**3 - fraction**2)
    return table


WIDTHS = [2 * (SUB - s) - (1 if f < 2 else 2) for s in range(SUB) for f in range(DYN)]
WIDTHS += [2 * SUB, 2 * SUB - 1]
PLANES = SUB * DYN
ITEMS = len(WIDTHS)
ROW_AT = np.concatenate([[0], np.cumsum(WIDTHS)]).tolist()
LANE_AT = ROW_AT[:ITEMS]
CORNERS = [max(w - 1, 0) for w in WIDTHS]
CORNER_AT = np.concatenate([[0], np.cumsum(CORNERS)]).tolist()
MAIN = -(-ROW_AT[-1] // 8) * 8
GROUPS = 2


def interp_kernel(table, mean, rows, first_ref, second_ref, out_ref, half_ref):
    part, levels, tiles, _ = first_ref.shape
    fields = part + second_ref.shape[0]
    for f in range(fields):
        level = [first_ref[f, k] if f < part else second_ref[f - part, k] for k in range(levels)]
        if f < DYN:
            for s in range(SUB):
                terms = [float(table[s, k]) * level[k] for k in range(levels) if table[s, k] != 0]
                out_ref[pl.ds(s * DYN + f, tiles, stride=rows), :] = functools.reduce(jnp.add, terms)
        else:
            terms = [float(mean[k]) * level[k] for k in range(levels)]
            out_ref[pl.ds(PLANES + f - DYN, tiles, stride=rows), :] = functools.reduce(jnp.add, terms)
    size = half_ref.shape[0]
    half_ref[...] = out_ref[pl.ds(pl.multiple_of(lax.axis_index("col") % 2 * size, 8), size), :]


def split_tiles(source_ref, split_ref, base, rows):
    tiles = source_ref.shape[0] // rows
    for g in range(tiles):
        value = source_ref[g * rows : min(g * rows + 32, source_ref.shape[0]), :]
        if value.shape[0] < 32:
            value = jnp.concatenate([value, jnp.zeros((32 - value.shape[0], value.shape[1]), value.dtype)], axis=0)
        high = value.astype(jnp.bfloat16)
        split_ref[base + g, 0:32, :] = high
        split_ref[base + g, 32:64, :] = (value - high.astype(jnp.float32)).astype(jnp.bfloat16)


def split_weights(wa, wb):
    weights = jnp.concatenate([wa, wb], axis=0)
    high = weights.astype(jnp.bfloat16)
    low = (weights - high.astype(jnp.float32)).astype(jnp.bfloat16)
    return jnp.concatenate([high, low], axis=1)


def remap_row(left, weights):
    both = jnp.dot(left, weights, preferred_element_type=jnp.float32)
    wide = weights.shape[1] // 2
    return both[0:32, :wide] + both[32:64, :wide] + both[0:32, wide:]


def own_kernel(rows, tiles_ref, own_ref, weight_ref, acc_ref, rest_ref, split_ref):
    index = tiles_ref[...] - split_ref.shape[0]
    split_tiles(own_ref, split_ref, 0, rows)
    for x in range(weight_ref.shape[0]):
        first, second = index[1, x], index[2, x]
        weights = split_weights(weight_ref[x, 1], weight_ref[x, 2])
        acc_ref[:, x, :] = remap_row(jnp.concatenate([split_ref[first], split_ref[second]], axis=1), weights)
        rest_ref[x] = split_weights(weight_ref[x, 0], weight_ref[x, 3])


def add_slot(rows, slot, offset, tiles_ref, near_ref, far_ref, rest_ref, add_ref, total_ref, split_ref):
    part = split_ref.shape[0] // 2
    split_tiles(near_ref, split_ref, 0, rows)
    split_tiles(far_ref, split_ref, part, rows)
    col_odd = lax.axis_index("col") % 2
    name = tiles_ref[...] - offset * 2 * part
    index = name % part + part * ((name // part + col_odd) % 2)
    cells = split_ref.shape[2]
    at = (slot > 0) * cells
    for x in range(rest_ref.shape[0]):
        total_ref[:, x, :] = remap_row(split_ref[index[slot, x]], rest_ref[x, at : at + cells, :]) + add_ref[:, x, :]


def first_push(force_ref, state_ref):
    zonal, merid = state_ref[1], state_ref[2]
    return zonal + 0.2 * merid + 0.5 * force_ref[0], merid + 0.5 * force_ref[1]


def rim_kernel(rows, tiles_ref, near_ref, far_ref, rest_ref, add_ref, state_ref, mask_ref,
               total_ref, down_ref, up_ref, edge1_ref, edge2_ref, split_ref):
    add_slot(rows, 3, 2, tiles_ref, near_ref, far_ref, rest_ref, add_ref, total_ref, split_ref)
    col_odd = lax.axis_index("col") % 2

    items = [*first_push(total_ref, state_ref)] + [total_ref[p] for p in range(2, PLANES)]
    items += [state_ref[0], mask_ref[...].astype(jnp.float32)]
    high, wide = mask_ref.shape
    col_even = col_odd == 0

    for i, value in enumerate(items):
        w, at = WIDTHS[i], ROW_AT[i]
        if w:
            down_ref[at : at + w, :] = value[high - w :]
            up_ref[at : at + w, :] = value[:w]
    for ref in (down_ref, up_ref):
        ref[ROW_AT[-1] :, :] = jnp.zeros((MAIN - ROW_AT[-1], wide), jnp.float32)

    lane = lax.broadcasted_iota(jnp.int32, (high, wide), 1)
    own = [(i, WIDTHS[i], WIDTHS[i], LANE_AT[i]) for i in range(ITEMS)]
    out = [(i, CORNERS[i], CORNERS[i], CORNER_AT[i]) for i in range(ITEMS)]
    for g, group in enumerate((own, out)):
        last = jnp.zeros((high, wide), jnp.float32)
        head = jnp.zeros((high, wide), jnp.float32)
        for i, count, w, at in group:
            if count:
                last = jnp.where(lane >= at, pltpu.roll(items[i], (at + w) % wide, 1), last)
                head = jnp.where(lane >= at, pltpu.roll(items[i], (at + count - w) % wide, 1), head)
        edge1_ref[g * high : (g + 1) * high, :] = jnp.where(col_even, last, head)
        edge2_ref[g * high : (g + 1) * high, :] = jnp.where(col_even, head, last)


def ocean_kernel(force_ref, state_ref, mask_ref, edge1_ref, edge2_ref, low_ref, corner_ref, top_ref, out_ref, *shift_refs):
    high, wide = mask_ref.shape
    col_even = lax.axis_index("col") % 2 == 0
    second = high + MAIN
    lane = lax.broadcasted_iota(jnp.int32, (high, wide), 1)

    def sides(a, b):
        return jnp.where(col_even, b, a), jnp.where(col_even, a, b)

    beside = sides(edge1_ref[:high], edge2_ref[:high])
    above = sides(corner_ref[:high], corner_ref[high:])
    below = sides(low_ref[:high], low_ref[second:])

    def edge(pair, w, at):
        left, right = pair
        if w == 0:
            return jnp.zeros_like(left)
        return jnp.where(lane < wide // 2, pltpu.roll(right, (wide - at) % wide, 1), pltpu.roll(left, (2 * wide - w - at) % wide, 1))

    def extended(i, own, rim):
        w, at = WIDTHS[i], ROW_AT[i]
        room = max(rim - at - w, 0)
        main = [jnp.zeros((room, wide), jnp.float32)] if room else []
        main += [top_ref[at + w - rim + room : at + w, :], own, low_ref[high + at : high + at + rim, :]]
        rest = [
            edge(above, CORNERS[i], CORNER_AT[i])[high - rim :],
            edge(beside, w, LANE_AT[i]),
            edge(below, CORNERS[i], CORNER_AT[i])[:rim],
        ]
        return [jnp.concatenate(main, axis=0), jnp.concatenate(rest, axis=0)]

    each = lambda f, *fields: [f(*parts) for parts in zip(*fields)]

    def slope_x(field, refs):
        out = []
        for ref, value in zip(refs, field):
            rows = value.shape[0]
            ref[8 : 8 + rows, :] = value
            out.append((ref[9 : 9 + rows, :] - ref[7 : 7 + rows, :]) * 0.5)
        return out

    def along(field, step):
        place = lax.broadcasted_iota(jnp.int32, field[0].shape, 1)
        crosses = place >= wide - step if step > 0 else place < -step
        moved = [pltpu.roll(v, -step % wide, 1) for v in field]
        return [jnp.where(crosses, moved[1], moved[0]), jnp.where(crosses, moved[0], moved[1])]

    def slope_y(field):
        return each(lambda a, b: (a - b) * 0.5, along(field, 1), along(field, -1))

    def slope_yy(field):
        return each(lambda a, v, b: ((a - v) - (v - b)) * 0.25, along(field, 2), field, along(field, -2))

    rim = high
    height = extended(PLANES, state_ref[0], rim)
    ocean = extended(PLANES + 1, mask_ref[...].astype(jnp.float32), rim)
    grad_y = slope_y(height)
    own = [*first_push(force_ref, state_ref)] + [force_ref[p] for p in range(2, PLANES)]
    for s in range(SUB):
        reach = -(-2 * (SUB - s) // 8) * 8
        if reach < rim:
            cut = rim - reach
            height, zonal, merid, ocean, grad_y = (
                each(lambda v: v[cut : v.shape[0] - cut], field) for field in (height, zonal, merid, ocean, grad_y)
            )
            rim = reach
        push_u, push_v, push_h = (extended(s * DYN + f, own[s * DYN + f], rim) for f in range(DYN))
        if s > 0:
            push_u = each(lambda u, v, p: u + 0.2 * v + 0.5 * p, zonal, merid, push_u)
            push_v = each(lambda v, p: v + 0.5 * p, merid, push_v)
        grad_x = slope_x(height, shift_refs[:2])
        zonal = each(lambda m, p, g: m * (p - g), ocean, push_u, grad_x)
        merid = each(lambda m, p, g, u: m * (p - g - 0.2 * u), ocean, push_v, grad_y, zonal)
        slope = slope_x(zonal, shift_refs[2:])
        spread = each(jnp.add, slope, slope_y(merid))
        height = each(lambda h, d, p: h - d + 0.5 * p, height, spread, push_h)
        if s < SUB - 1:
            rest = slope_y(each(lambda d, p: 0.5 * p - d, slope, push_h))
            grad_y = each(lambda g, r, b: g + r - b, grad_y, rest, slope_yy(merid))
    for k, value in enumerate((height, zonal, merid)):
        out_ref[k] = value[0][rim : rim + high]


def per_device(size_row, size_col, atmo_states, remap_weights, intersection_tiles, land_mask, ocean_state):
    fields, levels, tiles, cells = atmo_states.shape
    high, wide = land_mask.shape
    rows = PLANES + fields - DYN
    vmem = pl.BlockSpec(memory_space=pltpu.VMEM)
    f32 = lambda *shape: jax.ShapeDtypeStruct(shape, jnp.float32)
    params = lambda: pltpu.CompilerParams(vmem_limit_bytes=32 << 20)

    onward = [(i, (i + 1) % size_row) for i in range(size_row)]
    back = [(j, i) for i, j in onward]
    col_near = [(i, i ^ 1) for i in range(size_col)]
    col_far = [(i, (i + 1) % size_col if i % 2 else (i - 1) % size_col) for i in range(size_col)]
    half = tiles // 2
    names = intersection_tiles.T

    table = hermite_table(SUB, levels).astype(np.float32)
    mean = table.astype(np.float64).mean(axis=0)
    own, part = pl.pallas_call(
        functools.partial(interp_kernel, table, mean, rows),
        out_shape=(f32(tiles * rows, cells), f32(half * rows, cells)),
        in_specs=[vmem] * 2,
        out_specs=(vmem, vmem),
        compiler_params=params(),
        cost_estimate=pl.CostEstimate(flops=10**10, bytes_accessed=4 << 20, transcendentals=0),
    )(atmo_states[: fields // 2], atmo_states[fields // 2 :])
    previous = lax.ppermute(part, "row", onward)
    following = lax.ppermute(part, "row", back)

    acc, rest = pl.pallas_call(
        functools.partial(own_kernel, rows),
        out_shape=(f32(32, high, wide), jax.ShapeDtypeStruct((high, 2 * cells, 2 * wide), jnp.bfloat16)),
        in_specs=[vmem] * 3,
        out_specs=(vmem, vmem),
        scratch_shapes=[pltpu.VMEM((tiles, 64, cells), jnp.bfloat16)],
        compiler_params=params(),
        cost_estimate=pl.CostEstimate(flops=10**9, bytes_accessed=4 << 20, transcendentals=0),
    )(names, own, remap_weights)

    previous, acc, rest = lax.optimization_barrier((previous, acc, rest))
    previous_far = lax.ppermute(previous, "col", col_near)
    following_far = lax.ppermute(following, "col", col_near)
    acc = pl.pallas_call(
        functools.partial(add_slot, rows, 0, 0),
        out_shape=f32(32, high, wide),
        in_specs=[vmem] * 5,
        out_specs=vmem,
        scratch_shapes=[pltpu.VMEM((tiles, 64, cells), jnp.bfloat16)],
        compiler_params=params(),
        cost_estimate=pl.CostEstimate(flops=10**9, bytes_accessed=2 << 20, transcendentals=0),
    )(names, previous, previous_far, rest, acc)

    total, down, up, edge1, edge2 = pl.pallas_call(
        functools.partial(rim_kernel, rows),
        out_shape=(f32(32, high, wide), f32(MAIN, wide), f32(MAIN, wide), f32(GROUPS * high, wide), f32(GROUPS * high, wide)),
        in_specs=[vmem] * 7,
        out_specs=(vmem,) * 5,
        scratch_shapes=[pltpu.VMEM((tiles, 64, cells), jnp.bfloat16)],
        compiler_params=params(),
        cost_estimate=pl.CostEstimate(flops=10**9, bytes_accessed=4 << 20, transcendentals=0),
    )(names, following, following_far, rest, acc, ocean_state, land_mask)
    forced = total[:PLANES].reshape(SUB, DYN, high, wide)
    flux_mean = jnp.concatenate([jnp.mean(forced, axis=0), total[PLANES:rows]], axis=0)

    from1 = lax.ppermute(edge1, "col", col_near)
    from2 = lax.ppermute(edge2, "col", col_far)
    from2, from1 = lax.optimization_barrier((from2, from1))
    corners = from1[high:], from2[high:]
    top = lax.ppermute(down, "row", onward)
    corner = lax.ppermute(jnp.concatenate(corners), "row", onward)
    low = lax.ppermute(jnp.concatenate([corners[0], up, corners[1]]), "row", back)

    final = pl.pallas_call(
        ocean_kernel,
        out_shape=f32(3, high, wide),
        in_specs=[vmem] * 8,
        out_specs=vmem,
        scratch_shapes=[pltpu.VMEM((3 * high + 16, wide), jnp.float32)] * 4,
        compiler_params=params(),
    )(total, ocean_state, land_mask, from1, from2, low, corner, top)
    return flux_mean, final


def solution(mesh):
    placed = (
        P(None, None, "row", None),
        P("row", "col", None, None),
        P("row", "col"),
        P("row", "col"),
        P(None, "row", "col"),
    )
    return jax.shard_map(
        functools.partial(per_device, mesh.shape["row"], mesh.shape["col"]),
        mesh=mesh,
        in_specs=placed,
        out_specs=(P(None, "row", "col"), P(None, "row", "col")),
        check_vma=False,
    )
```

```python
import functools
import math

import jax
import jax.numpy as jnp
import numpy as np
from jax import lax
from jax.experimental import pallas as pl
from jax.experimental.pallas import tpu as pltpu
from jax.sharding import PartitionSpec as P

SUB = 6
DYN = 3


def hermite_table(count_sub, count_levels):
    table = np.zeros((count_sub, count_levels))

    def add_slope(position_row, level, factor):
        if level == 0:
            table[position_row, 1] += factor
            table[position_row, 0] -= factor
        elif level == count_levels - 1:
            table[position_row, level] += factor
            table[position_row, level - 1] -= factor
        else:
            table[position_row, level + 1] += 0.5 * factor
            table[position_row, level - 1] -= 0.5 * factor

    for substep in range(count_sub):
        position = (substep + 0.5) * (count_levels - 1) / count_sub
        lower = min(int(math.floor(position)), count_levels - 2)
        fraction = position - lower
        table[substep, lower] += 2 * fraction**3 - 3 * fraction**2 + 1
        table[substep, lower + 1] += -2 * fraction**3 + 3 * fraction**2
        add_slope(substep, lower, fraction**3 - 2 * fraction**2 + fraction)
        add_slope(substep, lower + 1, fraction**3 - fraction**2)
    return table


WIDTHS = [2 * (SUB - s) - (1 if f < 2 else 2) for s in range(SUB) for f in range(DYN)]
WIDTHS += [2 * SUB, 2 * SUB - 1]
PLANES = SUB * DYN
ITEMS = len(WIDTHS)
ROW_AT = np.concatenate([[0], np.cumsum(WIDTHS)]).tolist()
LANE_AT = ROW_AT[:ITEMS]
MAIN = -(-ROW_AT[-1] // 8) * 8


def interp_kernel(table, mean, rows, first_ref, second_ref, out_ref, half_ref):
    part, levels, tiles, _ = first_ref.shape
    fields = part + second_ref.shape[0]
    for f in range(fields):
        level = [first_ref[f, k] if f < part else second_ref[f - part, k] for k in range(levels)]
        if f < DYN:
            for s in range(SUB):
                terms = [float(table[s, k]) * level[k] for k in range(levels) if table[s, k] != 0]
                out_ref[pl.ds(s * DYN + f, tiles, stride=rows), :] = functools.reduce(jnp.add, terms)
        else:
            terms = [float(mean[k]) * level[k] for k in range(levels)]
            out_ref[pl.ds(PLANES + f - DYN, tiles, stride=rows), :] = functools.reduce(jnp.add, terms)
    size = half_ref.shape[0]
    half_ref[...] = out_ref[pl.ds(pl.multiple_of(lax.axis_index("col") % 2 * size, 8), size), :]


def split_tiles(source_ref, split_ref, base, rows):
    tiles = source_ref.shape[0] // rows
    for g in range(tiles):
        value = source_ref[g * rows : min(g * rows + 32, source_ref.shape[0]), :]
        if value.shape[0] < 32:
            value = jnp.concatenate([value, jnp.zeros((32 - value.shape[0], value.shape[1]), value.dtype)], axis=0)
        high = value.astype(jnp.bfloat16)
        split_ref[base + g, 0:32, :] = high
        split_ref[base + g, 32:64, :] = (value - high.astype(jnp.float32)).astype(jnp.bfloat16)


def split_weights(wa, wb):
    weights = jnp.concatenate([wa, wb], axis=0)
    high = weights.astype(jnp.bfloat16)
    low = (weights - high.astype(jnp.float32)).astype(jnp.bfloat16)
    return jnp.concatenate([high, low], axis=1)


def remap_row(left, weights):
    both = jnp.dot(left, weights, preferred_element_type=jnp.float32)
    wide = weights.shape[1] // 2
    return both[0:32, :wide] + both[32:64, :wide] + both[0:32, wide:]


def own_kernel(rows, tiles_ref, own_ref, weight_ref, acc_ref, rest_ref, split_ref):
    index = tiles_ref[...] - split_ref.shape[0]
    split_tiles(own_ref, split_ref, 0, rows)
    for x in range(weight_ref.shape[0]):
        first, second = index[1, x], index[2, x]
        weights = split_weights(weight_ref[x, 1], weight_ref[x, 2])
        acc_ref[:, x, :] = remap_row(jnp.concatenate([split_ref[first], split_ref[second]], axis=1), weights)
        rest_ref[x] = split_weights(weight_ref[x, 0], weight_ref[x, 3])


def add_slot(rows, slot, offset, tiles_ref, near_ref, far_ref, rest_ref, add_ref, total_ref, split_ref):
    part = split_ref.shape[0] // 2
    split_tiles(near_ref, split_ref, 0, rows)
    split_tiles(far_ref, split_ref, part, rows)
    col_odd = lax.axis_index("col") % 2
    name = tiles_ref[...] - offset * 2 * part
    index = name % part + part * ((name // part + col_odd) % 2)
    cells = split_ref.shape[2]
    at = (slot > 0) * cells
    for x in range(rest_ref.shape[0]):
        total_ref[:, x, :] = remap_row(split_ref[index[slot, x]], rest_ref[x, at : at + cells, :]) + add_ref[:, x, :]


def first_push(force_ref, state_ref):
    zonal, merid = state_ref[1], state_ref[2]
    return zonal + 0.2 * merid + 0.5 * force_ref[0], merid + 0.5 * force_ref[1]


def rim_kernel(rows, tiles_ref, near_ref, far_ref, rest_ref, add_ref, state_ref, mask_ref,
               total_ref, down_ref, up_ref, edge1_ref, edge2_ref, split_ref):
    add_slot(rows, 3, 2, tiles_ref, near_ref, far_ref, rest_ref, add_ref, total_ref, split_ref)
    col_odd = lax.axis_index("col") % 2

    items = [*first_push(total_ref, state_ref)] + [total_ref[p] for p in range(2, PLANES)]
    items += [state_ref[0], mask_ref[...].astype(jnp.float32)]
    high, wide = mask_ref.shape
    col_even = col_odd == 0

    for i, value in enumerate(items):
        w, at = WIDTHS[i], ROW_AT[i]
        if w:
            down_ref[at : at + w, :] = value[high - w :]
            up_ref[at : at + w, :] = value[:w]
    for ref in (down_ref, up_ref):
        ref[ROW_AT[-1] :, :] = jnp.zeros((MAIN - ROW_AT[-1], wide), jnp.float32)

    lane = lax.broadcasted_iota(jnp.int32, (high, wide), 1)
    last = jnp.zeros((high, wide), jnp.float32)
    head = jnp.zeros((high, wide), jnp.float32)
    for value, w, at in zip(items, WIDTHS, LANE_AT):
        if w:
            last = jnp.where(lane >= at, pltpu.roll(value, (at + w) % wide, 1), last)
            head = jnp.where(lane >= at, pltpu.roll(value, at, 1), head)
    edge1_ref[...] = jnp.where(col_even, last, head)
    edge2_ref[...] = jnp.where(col_even, head, last)


def ocean_kernel(force_ref, state_ref, mask_ref, edge1_ref, edge2_ref, low_ref, corner_ref, top_ref, out_ref, *shift_refs):
    high, wide = mask_ref.shape
    col_even = lax.axis_index("col") % 2 == 0
    second = high + MAIN
    lane = lax.broadcasted_iota(jnp.int32, (high, wide), 1)

    def sides(a, b):
        return jnp.where(col_even, b, a), jnp.where(col_even, a, b)

    beside = sides(edge1_ref[...], edge2_ref[...])
    above = sides(corner_ref[:high], corner_ref[high:])
    below = sides(low_ref[:high], low_ref[second:])

    def edge(pair, w, at):
        left, right = pair
        if w == 0:
            return jnp.zeros_like(left)
        return jnp.where(lane < wide // 2, pltpu.roll(right, (wide - at) % wide, 1), pltpu.roll(left, (2 * wide - w - at) % wide, 1))

    def extended(i, own, rim):
        w, at = WIDTHS[i], ROW_AT[i]
        room = max(rim - at - w, 0)
        main = [jnp.zeros((room, wide), jnp.float32)] if room else []
        main += [top_ref[at + w - rim + room : at + w, :], own, low_ref[high + at : high + at + rim, :]]
        rest = [
            edge(above, w, LANE_AT[i])[high - rim :],
            edge(beside, w, LANE_AT[i]),
            edge(below, w, LANE_AT[i])[:rim],
        ]
        return [jnp.concatenate(main, axis=0), jnp.concatenate(rest, axis=0)]

    each = lambda f, *fields: [f(*parts) for parts in zip(*fields)]

    def slope_x(field, refs):
        out = []
        for ref, value in zip(refs, field):
            rows = value.shape[0]
            ref[8 : 8 + rows, :] = value
            out.append((ref[9 : 9 + rows, :] - ref[7 : 7 + rows, :]) * 0.5)
        return out

    def along(field, step):
        place = lax.broadcasted_iota(jnp.int32, field[0].shape, 1)
        crosses = place >= wide - step if step > 0 else place < -step
        moved = [pltpu.roll(v, -step % wide, 1) for v in field]
        return [jnp.where(crosses, moved[1], moved[0]), jnp.where(crosses, moved[0], moved[1])]

    def slope_y(field):
        return each(lambda a, b: (a - b) * 0.5, along(field, 1), along(field, -1))

    def slope_yy(field):
        return each(lambda a, v, b: ((a - v) - (v - b)) * 0.25, along(field, 2), field, along(field, -2))

    rim = high
    height = extended(PLANES, state_ref[0], rim)
    ocean = extended(PLANES + 1, mask_ref[...].astype(jnp.float32), rim)
    grad_y = slope_y(height)
    own = [*first_push(force_ref, state_ref)] + [force_ref[p] for p in range(2, PLANES)]
    for s in range(SUB):
        reach = -(-2 * (SUB - s) // 8) * 8
        if reach < rim:
            cut = rim - reach
            height, zonal, merid, ocean, grad_y = (
                each(lambda v: v[cut : v.shape[0] - cut], field) for field in (height, zonal, merid, ocean, grad_y)
            )
            rim = reach
        push_u, push_v, push_h = (extended(s * DYN + f, own[s * DYN + f], rim) for f in range(DYN))
        if s > 0:
            push_u = each(lambda u, v, p: u + 0.2 * v + 0.5 * p, zonal, merid, push_u)
            push_v = each(lambda v, p: v + 0.5 * p, merid, push_v)
        grad_x = slope_x(height, shift_refs[:2])
        zonal = each(lambda m, p, g: m * (p - g), ocean, push_u, grad_x)
        merid = each(lambda m, p, g, u: m * (p - g - 0.2 * u), ocean, push_v, grad_y, zonal)
        slope = slope_x(zonal, shift_refs[2:])
        spread = each(jnp.add, slope, slope_y(merid))
        height = each(lambda h, d, p: h - d + 0.5 * p, height, spread, push_h)
        if s < SUB - 1:
            rest = slope_y(each(lambda d, p: 0.5 * p - d, slope, push_h))
            grad_y = each(lambda g, r, b: g + r - b, grad_y, rest, slope_yy(merid))
    for k, value in enumerate((height, zonal, merid)):
        out_ref[k] = value[0][rim : rim + high]


def per_device(size_row, size_col, atmo_states, remap_weights, intersection_tiles, land_mask, ocean_state):
    fields, levels, tiles, cells = atmo_states.shape
    high, wide = land_mask.shape
    rows = PLANES + fields - DYN
    vmem = pl.BlockSpec(memory_space=pltpu.VMEM)
    f32 = lambda *shape: jax.ShapeDtypeStruct(shape, jnp.float32)
    params = lambda: pltpu.CompilerParams(vmem_limit_bytes=32 << 20)

    onward = [(i, (i + 1) % size_row) for i in range(size_row)]
    back = [(j, i) for i, j in onward]
    col_near = [(i, i ^ 1) for i in range(size_col)]
    col_far = [(i, (i + 1) % size_col if i % 2 else (i - 1) % size_col) for i in range(size_col)]
    half = tiles // 2
    names = intersection_tiles.T

    table = hermite_table(SUB, levels).astype(np.float32)
    mean = table.astype(np.float64).mean(axis=0)
    own, part = pl.pallas_call(
        functools.partial(interp_kernel, table, mean, rows),
        out_shape=(f32(tiles * rows, cells), f32(half * rows, cells)),
        in_specs=[vmem] * 2,
        out_specs=(vmem, vmem),
        compiler_params=params(),
        cost_estimate=pl.CostEstimate(flops=10**10, bytes_accessed=4 << 20, transcendentals=0),
    )(atmo_states[: fields // 2], atmo_states[fields // 2 :])
    previous = lax.ppermute(part, "row", onward)
    following = lax.ppermute(part, "row", back)

    acc, rest = pl.pallas_call(
        functools.partial(own_kernel, rows),
        out_shape=(f32(32, high, wide), jax.ShapeDtypeStruct((high, 2 * cells, 2 * wide), jnp.bfloat16)),
        in_specs=[vmem] * 3,
        out_specs=(vmem, vmem),
        scratch_shapes=[pltpu.VMEM((tiles, 64, cells), jnp.bfloat16)],
        compiler_params=params(),
        cost_estimate=pl.CostEstimate(flops=10**9, bytes_accessed=4 << 20, transcendentals=0),
    )(names, own, remap_weights)

    previous, acc, rest = lax.optimization_barrier((previous, acc, rest))
    previous_far = lax.ppermute(previous, "col", col_near)
    following_far = lax.ppermute(following, "col", col_near)
    acc = pl.pallas_call(
        functools.partial(add_slot, rows, 0, 0),
        out_shape=f32(32, high, wide),
        in_specs=[vmem] * 5,
        out_specs=vmem,
        scratch_shapes=[pltpu.VMEM((tiles, 64, cells), jnp.bfloat16)],
        compiler_params=params(),
        cost_estimate=pl.CostEstimate(flops=10**9, bytes_accessed=2 << 20, transcendentals=0),
    )(names, previous, previous_far, rest, acc)

    total, down, up, edge1, edge2 = pl.pallas_call(
        functools.partial(rim_kernel, rows),
        out_shape=(f32(32, high, wide), f32(MAIN, wide), f32(MAIN, wide), f32(high, wide), f32(high, wide)),
        in_specs=[vmem] * 7,
        out_specs=(vmem,) * 5,
        scratch_shapes=[pltpu.VMEM((tiles, 64, cells), jnp.bfloat16)],
        compiler_params=params(),
        cost_estimate=pl.CostEstimate(flops=10**9, bytes_accessed=4 << 20, transcendentals=0),
    )(names, following, following_far, rest, acc, ocean_state, land_mask)
    forced = total[:PLANES].reshape(SUB, DYN, high, wide)
    flux_mean = jnp.concatenate([jnp.mean(forced, axis=0), total[PLANES:rows]], axis=0)

    from1 = lax.ppermute(edge1, "col", col_near)
    from2 = lax.ppermute(edge2, "col", col_far)
    from2, from1 = lax.optimization_barrier((from2, from1))
    corners = from1, from2
    top = lax.ppermute(down, "row", onward)
    corner = lax.ppermute(jnp.concatenate(corners), "row", onward)
    low = lax.ppermute(jnp.concatenate([corners[0], up, corners[1]]), "row", back)

    final = pl.pallas_call(
        ocean_kernel,
        out_shape=f32(3, high, wide),
        in_specs=[vmem] * 8,
        out_specs=vmem,
        scratch_shapes=[pltpu.VMEM((3 * high + 16, wide), jnp.float32)] * 4,
        compiler_params=params(),
    )(total, ocean_state, land_mask, from1, from2, low, corner, top)
    return flux_mean, final


def solution(mesh):
    placed = (
        P(None, None, "row", None),
        P("row", "col", None, None),
        P("row", "col"),
        P("row", "col"),
        P(None, "row", "col"),
    )
    return jax.shard_map(
        functools.partial(per_device, mesh.shape["row"], mesh.shape["col"]),
        mesh=mesh,
        in_specs=placed,
        out_specs=(P(None, "row", "col"), P(None, "row", "col")),
        check_vma=False,
    )
```

```python
import functools
import math

import jax
import jax.numpy as jnp
import numpy as np
from jax import lax
from jax.experimental import pallas as pl
from jax.experimental.pallas import tpu as pltpu
from jax.sharding import PartitionSpec as P

SUB = 6
DYN = 3


def hermite_table(count_sub, count_levels):
    table = np.zeros((count_sub, count_levels))

    def add_slope(position_row, level, factor):
        if level == 0:
            table[position_row, 1] += factor
            table[position_row, 0] -= factor
        elif level == count_levels - 1:
            table[position_row, level] += factor
            table[position_row, level - 1] -= factor
        else:
            table[position_row, level + 1] += 0.5 * factor
            table[position_row, level - 1] -= 0.5 * factor

    for substep in range(count_sub):
        position = (substep + 0.5) * (count_levels - 1) / count_sub
        lower = min(int(math.floor(position)), count_levels - 2)
        fraction = position - lower
        table[substep, lower] += 2 * fraction**3 - 3 * fraction**2 + 1
        table[substep, lower + 1] += -2 * fraction**3 + 3 * fraction**2
        add_slope(substep, lower, fraction**3 - 2 * fraction**2 + fraction)
        add_slope(substep, lower + 1, fraction**3 - fraction**2)
    return table


WIDTHS = [2 * (SUB - s) - (1 if f < 2 else 2) for s in range(SUB) for f in range(DYN)]
WIDTHS += [2 * SUB, 2 * SUB - 1]
PLANES = SUB * DYN
ITEMS = len(WIDTHS)
ROW_AT = np.concatenate([[0], np.cumsum(WIDTHS)]).tolist()
LANE_AT = ROW_AT[:ITEMS]
MAIN = -(-ROW_AT[-1] // 8) * 8


def interp_kernel(table, mean, rows, first_ref, second_ref, out_ref, half_ref):
    part, levels, tiles, _ = first_ref.shape
    fields = part + second_ref.shape[0]
    for f in range(fields):
        level = [first_ref[f, k] if f < part else second_ref[f - part, k] for k in range(levels)]
        if f < DYN:
            for s in range(SUB):
                terms = [float(table[s, k]) * level[k] for k in range(levels) if table[s, k] != 0]
                out_ref[pl.ds(s * DYN + f, tiles, stride=rows), :] = functools.reduce(jnp.add, terms)
        else:
            terms = [float(mean[k]) * level[k] for k in range(levels)]
            out_ref[pl.ds(PLANES + f - DYN, tiles, stride=rows), :] = functools.reduce(jnp.add, terms)
    size = half_ref.shape[0]
    half_ref[...] = out_ref[pl.ds(pl.multiple_of(lax.axis_index("col") % 2 * size, 8), size), :]


def split_tiles(source_ref, split_ref, base, rows):
    tiles = source_ref.shape[0] // rows
    for g in range(tiles):
        value = source_ref[g * rows : min(g * rows + 32, source_ref.shape[0]), :]
        if value.shape[0] < 32:
            value = jnp.concatenate([value, jnp.zeros((32 - value.shape[0], value.shape[1]), value.dtype)], axis=0)
        high = value.astype(jnp.bfloat16)
        split_ref[base + g, 0:32, :] = high
        split_ref[base + g, 32:64, :] = (value - high.astype(jnp.float32)).astype(jnp.bfloat16)


def split_weights(wa, wb):
    weights = jnp.concatenate([wa, wb], axis=0)
    high = weights.astype(jnp.bfloat16)
    low = (weights - high.astype(jnp.float32)).astype(jnp.bfloat16)
    return jnp.concatenate([high, low], axis=1)


def remap_row(left, weights):
    both = jnp.dot(left, weights, preferred_element_type=jnp.float32)
    wide = weights.shape[1] // 2
    return both[0:32, :wide] + both[32:64, :wide] + both[0:32, wide:]


def own_kernel(rows, tiles_ref, own_ref, weight_ref, acc_ref, rest_ref, split_ref):
    index = tiles_ref[...] - split_ref.shape[0]
    cells = weight_ref.shape[2]
    split_tiles(own_ref, split_ref, 0, rows)
    for x in range(weight_ref.shape[0]):
        first, second = index[1, x], index[2, x]
        weights = split_weights(weight_ref[x, 1], weight_ref[x, 2])
        acc_ref[:, x, :] = remap_row(jnp.concatenate([split_ref[first], split_ref[second]], axis=1), weights)
        for k, slot in enumerate((0, 3)):
            high = weight_ref[x, slot].astype(jnp.bfloat16)
            low = (weight_ref[x, slot] - high.astype(jnp.float32)).astype(jnp.bfloat16)
            rest_ref[x, 2 * k * cells : 2 * (k + 1) * cells, :] = jnp.concatenate([high, low], axis=0)


def add_slot(rows, slot, offset, tiles_ref, near_ref, far_ref, rest_ref, add_ref, total_ref, split_ref):
    part = split_ref.shape[0] // 2
    split_tiles(near_ref, split_ref, 0, rows)
    split_tiles(far_ref, split_ref, part, rows)
    col_odd = lax.axis_index("col") % 2
    name = tiles_ref[...] - offset * 2 * part
    index = name % part + part * ((name // part + col_odd) % 2)
    cells = split_ref.shape[2]
    at = (slot > 0) * 2 * cells
    for x in range(rest_ref.shape[0]):
        tile = split_ref[index[slot, x]]
        upper = jnp.concatenate([tile[0:32], tile[0:32]], axis=1)
        lower = jnp.concatenate([tile[32:64], jnp.zeros_like(tile[32:64])], axis=1)
        left = jnp.concatenate([upper, lower], axis=0)
        both = jnp.dot(left, rest_ref[x, at : at + 2 * cells, :], preferred_element_type=jnp.float32)
        total_ref[:, x, :] = both[0:32] + both[32:64] + add_ref[:, x, :]


def first_push(force_ref, state_ref):
    zonal, merid = state_ref[1], state_ref[2]
    return zonal + 0.2 * merid + 0.5 * force_ref[0], merid + 0.5 * force_ref[1]


def rim_kernel(rows, tiles_ref, near_ref, far_ref, rest_ref, add_ref, state_ref, mask_ref,
               total_ref, down_ref, up_ref, edge1_ref, edge2_ref, split_ref):
    add_slot(rows, 3, 2, tiles_ref, near_ref, far_ref, rest_ref, add_ref, total_ref, split_ref)
    col_odd = lax.axis_index("col") % 2

    items = [*first_push(total_ref, state_ref)] + [total_ref[p] for p in range(2, PLANES)]
    items += [state_ref[0], mask_ref[...].astype(jnp.float32)]
    high, wide = mask_ref.shape
    col_even = col_odd == 0

    for i, value in enumerate(items):
        w, at = WIDTHS[i], ROW_AT[i]
        if w:
            down_ref[at : at + w, :] = value[high - w :]
            up_ref[at : at + w, :] = value[:w]
    for ref in (down_ref, up_ref):
        ref[ROW_AT[-1] :, :] = jnp.zeros((MAIN - ROW_AT[-1], wide), jnp.float32)

    lane = lax.broadcasted_iota(jnp.int32, (high, wide), 1)
    last = jnp.zeros((high, wide), jnp.float32)
    head = jnp.zeros((high, wide), jnp.float32)
    for value, w, at in zip(items, WIDTHS, LANE_AT):
        if w:
            last = jnp.where(lane >= at, pltpu.roll(value, (at + w) % wide, 1), last)
            head = jnp.where(lane >= at, pltpu.roll(value, at, 1), head)
    edge1_ref[...] = jnp.where(col_even, last, head)
    edge2_ref[...] = jnp.where(col_even, head, last)


def ocean_kernel(force_ref, state_ref, mask_ref, edge1_ref, edge2_ref, low_ref, corner_ref, top_ref, out_ref, held_ref, sems, *shift_refs):
    high, wide = mask_ref.shape
    col_even = lax.axis_index("col") % 2 == 0
    second = high + MAIN
    lane = lax.broadcasted_iota(jnp.int32, (high, wide), 1)

    def sides(a, b):
        return jnp.where(col_even, b, a), jnp.where(col_even, a, b)

    beside = sides(edge1_ref[...], edge2_ref[...])
    above = sides(corner_ref[:high], corner_ref[high:])
    below = sides(low_ref[:high], low_ref[second:])

    def edge(pair, w, at):
        left, right = pair
        if w == 0:
            return jnp.zeros_like(left)
        return jnp.where(lane < wide // 2, pltpu.roll(right, (wide - at) % wide, 1), pltpu.roll(left, (2 * wide - w - at) % wide, 1))

    def extended(i, own, rim):
        w, at = WIDTHS[i], ROW_AT[i]
        room = max(rim - at - w, 0)
        main = [jnp.zeros((room, wide), jnp.float32)] if room else []
        main += [top_ref[at + w - rim + room : at + w, :], own, low_ref[high + at : high + at + rim, :]]
        rest = [
            edge(above, w, LANE_AT[i])[high - rim :],
            edge(beside, w, LANE_AT[i]),
            edge(below, w, LANE_AT[i])[:rim],
        ]
        return [jnp.concatenate(main, axis=0), jnp.concatenate(rest, axis=0)]

    each = lambda f, *fields: [f(*parts) for parts in zip(*fields)]

    def slope_x(field, refs):
        out = []
        for ref, value in zip(refs, field):
            rows = value.shape[0]
            ref[8 : 8 + rows, :] = value
            out.append((ref[9 : 9 + rows, :] - ref[7 : 7 + rows, :]) * 0.5)
        return out

    def along(field, step):
        place = lax.broadcasted_iota(jnp.int32, field[0].shape, 1)
        crosses = place >= wide - step if step > 0 else place < -step
        moved = [pltpu.roll(v, -step % wide, 1) for v in field]
        return [jnp.where(crosses, moved[1], moved[0]), jnp.where(crosses, moved[0], moved[1])]

    def slope_y(field):
        return each(lambda a, b: (a - b) * 0.5, along(field, 1), along(field, -1))

    def slope_yy(field):
        return each(lambda a, v, b: ((a - v) - (v - b)) * 0.25, along(field, 2), field, along(field, -2))

    rim = high
    height = extended(PLANES, state_ref[0], rim)
    ocean = extended(PLANES + 1, mask_ref[...].astype(jnp.float32), rim)
    grad_y = slope_y(height)
    own = [*first_push(force_ref, state_ref)] + [force_ref[p] for p in range(2, PLANES)]
    for s in range(SUB):
        reach = -(-2 * (SUB - s) // 8) * 8
        if reach < rim:
            cut = rim - reach
            height, zonal, merid, ocean, grad_y = (
                each(lambda v: v[cut : v.shape[0] - cut], field) for field in (height, zonal, merid, ocean, grad_y)
            )
            rim = reach
        push_u, push_v, push_h = (extended(s * DYN + f, own[s * DYN + f], rim) for f in range(DYN))
        if s > 0:
            push_u = each(lambda u, v, p: u + 0.2 * v + 0.5 * p, zonal, merid, push_u)
            push_v = each(lambda v, p: v + 0.5 * p, merid, push_v)
        grad_x = slope_x(height, shift_refs[:2])
        zonal = each(lambda m, p, g: m * (p - g), ocean, push_u, grad_x)
        merid = each(lambda m, p, g, u: m * (p - g - 0.2 * u), ocean, push_v, grad_y, zonal)
        if s == SUB - 1:
            for k, value in ((1, zonal), (2, merid)):
                held_ref[k] = value[0][rim : rim + high]
                pltpu.make_async_copy(held_ref.at[k], out_ref.at[k], sems.at[k]).start()
        slope = slope_x(zonal, shift_refs[2:])
        spread = each(jnp.add, slope, slope_y(merid))
        height = each(lambda h, d, p: h - d + 0.5 * p, height, spread, push_h)
        if s < SUB - 1:
            rest = slope_y(each(lambda d, p: 0.5 * p - d, slope, push_h))
            grad_y = each(lambda g, r, b: g + r - b, grad_y, rest, slope_yy(merid))
    held_ref[0] = height[0][rim : rim + high]
    pltpu.make_async_copy(held_ref.at[0], out_ref.at[0], sems.at[0]).start()
    for k in range(3):
        pltpu.make_async_copy(held_ref.at[k], out_ref.at[k], sems.at[k]).wait()


def per_device(size_row, size_col, atmo_states, remap_weights, intersection_tiles, land_mask, ocean_state):
    fields, levels, tiles, cells = atmo_states.shape
    high, wide = land_mask.shape
    rows = PLANES + fields - DYN
    vmem = pl.BlockSpec(memory_space=pltpu.VMEM)
    f32 = lambda *shape: jax.ShapeDtypeStruct(shape, jnp.float32)
    params = lambda: pltpu.CompilerParams(vmem_limit_bytes=32 << 20)

    onward = [(i, (i + 1) % size_row) for i in range(size_row)]
    back = [(j, i) for i, j in onward]
    col_near = [(i, i ^ 1) for i in range(size_col)]
    col_far = [(i, (i + 1) % size_col if i % 2 else (i - 1) % size_col) for i in range(size_col)]
    half = tiles // 2
    names = intersection_tiles.T

    table = hermite_table(SUB, levels).astype(np.float32)
    mean = table.astype(np.float64).mean(axis=0)
    own, part = pl.pallas_call(
        functools.partial(interp_kernel, table, mean, rows),
        out_shape=(f32(tiles * rows, cells), f32(half * rows, cells)),
        in_specs=[vmem] * 2,
        out_specs=(vmem, vmem),
        compiler_params=params(),
        cost_estimate=pl.CostEstimate(flops=10**10, bytes_accessed=4 << 20, transcendentals=0),
    )(atmo_states[: fields // 2], atmo_states[fields // 2 :])
    previous = lax.ppermute(part, "row", onward)
    following = lax.ppermute(part, "row", back)

    acc, rest = pl.pallas_call(
        functools.partial(own_kernel, rows),
        out_shape=(f32(32, high, wide), jax.ShapeDtypeStruct((high, 4 * cells, wide), jnp.bfloat16)),
        in_specs=[vmem] * 3,
        out_specs=(vmem, vmem),
        scratch_shapes=[pltpu.VMEM((tiles, 64, cells), jnp.bfloat16)],
        compiler_params=params(),
        cost_estimate=pl.CostEstimate(flops=10**9, bytes_accessed=4 << 20, transcendentals=0),
    )(names, own, remap_weights)

    previous, acc, rest = lax.optimization_barrier((previous, acc, rest))
    previous_far = lax.ppermute(previous, "col", col_near)
    following_far = lax.ppermute(following, "col", col_near)
    acc = pl.pallas_call(
        functools.partial(add_slot, rows, 0, 0),
        out_shape=f32(32, high, wide),
        in_specs=[vmem] * 5,
        out_specs=vmem,
        scratch_shapes=[pltpu.VMEM((tiles, 64, cells), jnp.bfloat16)],
        compiler_params=params(),
        cost_estimate=pl.CostEstimate(flops=10**9, bytes_accessed=2 << 20, transcendentals=0),
    )(names, previous, previous_far, rest, acc)

    total, down, up, edge1, edge2 = pl.pallas_call(
        functools.partial(rim_kernel, rows),
        out_shape=(f32(32, high, wide), f32(MAIN, wide), f32(MAIN, wide), f32(high, wide), f32(high, wide)),
        in_specs=[vmem] * 7,
        out_specs=(vmem,) * 5,
        scratch_shapes=[pltpu.VMEM((tiles, 64, cells), jnp.bfloat16)],
        compiler_params=params(),
        cost_estimate=pl.CostEstimate(flops=10**9, bytes_accessed=4 << 20, transcendentals=0),
    )(names, following, following_far, rest, acc, ocean_state, land_mask)
    forced = total[:PLANES].reshape(SUB, DYN, high, wide)
    flux_mean = jnp.concatenate([jnp.mean(forced, axis=0), total[PLANES:rows]], axis=0)

    from1 = lax.ppermute(edge1, "col", col_near)
    from2 = lax.ppermute(edge2, "col", col_far)
    from2, from1 = lax.optimization_barrier((from2, from1))
    corners = from1, from2
    top = lax.ppermute(down, "row", onward)
    corner = lax.ppermute(jnp.concatenate(corners), "row", onward)
    low = lax.ppermute(jnp.concatenate([corners[0], up, corners[1]]), "row", back)

    final = pl.pallas_call(
        ocean_kernel,
        out_shape=f32(3, high, wide),
        in_specs=[vmem] * 8,
        out_specs=pl.BlockSpec(memory_space=pl.ANY),
        scratch_shapes=[pltpu.VMEM((3, high, wide), jnp.float32), pltpu.SemaphoreType.DMA((3,))]
        + [pltpu.VMEM((3 * high + 16, wide), jnp.float32)] * 4,
        compiler_params=params(),
    )(total, ocean_state, land_mask, from1, from2, low, corner, top)
    return flux_mean, final


def solution(mesh):
    placed = (
        P(None, None, "row", None),
        P("row", "col", None, None),
        P("row", "col"),
        P("row", "col"),
        P(None, "row", "col"),
    )
    return jax.shard_map(
        functools.partial(per_device, mesh.shape["row"], mesh.shape["col"]),
        mesh=mesh,
        in_specs=placed,
        out_specs=(P(None, "row", "col"), P(None, "row", "col")),
        check_vma=False,
    )
```
